32 devices in a mesh: rep: 2 (over y), fast: 16 (over z, x, core).
Axes of the slice: x: 2, y: 2, z: 4, core: 2. Of those that a mesh axis runs over, the one named last changes fastest.
Arguments:
- tokens: bfloat16 [2, 128, 7168], P(None, ('rep', 'fast')), parts along dimension 1, may hold values from -6 to 6
- expert_ids: int32 [2, 128, 3], P(None, ('rep', 'fast')), parts along dimension 1, may hold values from 0 to 7, all different within a row; in each aligned block of 4 rows (0 to 3, 4 to 7, ..., all dimensions but the last counted through in order) at most 2 rows name the same one
- gate_weights: bfloat16 [2, 128, 3], P(None, ('rep', 'fast')), parts along dimension 1, may hold values from 0.19921875 to 1
- w_gate_up: bfloat16 [7168, 2, 16384], P(None, None, 'fast'), may hold values from -0.0625 to 0.0625
- w_down: bfloat16 [16384, 7168], P('fast'), may hold values from -0.125 to 0.125
- shared_gate_up: bfloat16 [7168, 2, 16384], P(None, None, 'fast'), as said below
- shared_down: bfloat16 [16384, 7168], P('fast'), as said below
Outputs:
- mixed: bfloat16 [2, 128, 7168], P(None, ('rep', 'fast')), parts along dimension 1
The draws below stay inside these ranges and needn't reach their ends.
There are 2 independent parts, one for each index of `rep`. The reference program is written for one: setup_inputs(seed, part) draws one part's arguments, and reference() takes and returns one part's arrays. A program takes and returns all parts, laid end to end along the dimension named above; an argument that names none is the same for every part. Nothing has to cross between parts.
Inputs may be any that keep to these rules, and one draw needn't show every extreme that they name: `expert_ids`: the 3 ids of a token differ. Of the 4 tokens that one device holds in one decode step (an aligned block of rows), at most 2 name one expert, and in every draw some expert is named by exactly 2 of them. `shared_gate_up`: the 8 blocks of 2048 columns are equal copies of one shared expert. `shared_down`: the 8 blocks of 2048 rows are equal copies of one shared expert.
All inputs are finite; a program needn't handle non-finite values.
Results may differ from the reference program's by a relative error of at most 0.0058.
Values may be sent and summed in bfloat16 or wider, within the bound.
A program may use at most 192 MiB of HBM per device.

```python
import math
import jax
import jax.numpy as jnp
import numpy as np
from jax import lax

D = 7168
FF = 2048
EXPERTS = 8
TOPK = 3
STEPS = 2
TOK_STEP = 4
CAP = 2
TOKENS = 64
N_FAST = 16


def draw_shared_gate_up(key, part):
    base = jnp.clip(jax.random.normal(key, (D, 2, FF), jnp.float32), -6.0, 6.0)
    base = base * D ** (-0.5)
    return jnp.tile(base, (1, 1, EXPERTS)).astype(jnp.bfloat16)


def draw_shared_down(key, part):
    base = jnp.clip(jax.random.normal(key, (FF, D), jnp.float32), -6.0, 6.0)
    base = base * FF ** (-0.5)
    return jnp.tile(base, (EXPERTS, 1)).astype(jnp.bfloat16)


def block_scale(rng, extent, split, least, largest):
    level = 1.0
    for dim, parts in split:
        steps = jax.random.uniform(jax.random.fold_in(jax.random.fold_in(rng, 6), dim), (parts,), jnp.float32, least / len(split), largest / len(split))
        level = level * jnp.repeat(jnp.exp(steps), extent[dim] // parts).reshape((-1,) + (1,) * (len(extent) - 1 - dim))
    return level


def routed_block(rng, own, number, rows, number_of, top, reach, slope):
    ranking = jax.random.permutation(rng, number_of)
    heavy_load, usual = shares(number_of, rows * top, reach, slope, True), shares(number_of, rows * top, reach, slope, False)
    places = jnp.arange(number_of)

    def named(sizes, offset_by):
        used = int((sizes > 0).sum())
        fixed = max(1, used // 4)
        shifted = fixed + (places - fixed + offset_by * (used - fixed)) % max(1, number_of - fixed)
        return jnp.zeros((number_of,), jnp.int32).at[ranking[jnp.where(places < fixed, places, shifted)]].set(jnp.asarray(sizes, jnp.int32))

    sizes = jnp.where(number % 4 == 0, named(heavy_load, number // 4), named(usual, number - number // 4 - 1))
    mixed = jax.random.permutation(jax.random.fold_in(own, 3), number_of)
    donor, receiver = mixed[0:number_of // 2 * 2:2], mixed[1:number_of // 2 * 2:2]
    room = jnp.minimum(sizes[donor] - 1, reach - sizes[receiver]) // 2
    room = jnp.where((donor == ranking[0]) | (receiver == ranking[0]) | (sizes[receiver] == 0), 0, jnp.maximum(room, 0))
    shifted = jax.random.randint(jax.random.fold_in(own, 4), (number_of // 2,), 0, 1 << 20) % (room + 1)
    sizes = sizes.at[donor].add(-shifted).at[receiver].add(shifted)
    members = jnp.searchsorted(jnp.cumsum(sizes), jnp.arange(rows * top), side="right").astype(jnp.int32)
    grid = members.reshape(top, rows).T
    grid = grid[jax.random.permutation(jax.random.fold_in(own, 1), rows)]
    offset_by = jax.random.randint(jax.random.fold_in(own, 2), (rows, 1), 0, top)
    return jnp.take_along_axis(grid, (jnp.arange(top)[None, :] + offset_by) % top, axis=1)


def shares(amount, total, most, skew, full):
    portions = [(1 << 20) // math.isqrt(grade ** skew) + 1 for grade in range(1, amount + 1)]
    largest = most if full else min(most, max(-(-total // amount), total * portions[0] // sum(portions)))
    least = 1 if total - largest >= amount - 1 else 0
    given, spare = [largest] + [least] * (amount - 1), total - largest - least * (amount - 1)
    while spare > 0:
        movable = [i for i in range(1, amount) if given[i] < largest] or [i for i in range(1, amount) if given[i] < most]
        mass, budget = sum([portions[i] for i in movable]), spare
        for i in movable:
            addition = min(most - given[i], max(1, budget * portions[i] // mass), spare)
            given[i] = given[i] + addition
            spare = spare - addition
    return np.array(given)


def normal_values(stream_key, dims, scale, most, shards=(), held_as=jnp.bfloat16):
    entries = scale * jax.random.normal(stream_key, dims, jnp.float32)
    if shards:
        entries = entries * block_scale(stream_key, dims, shards, -0.22, 0.18)
    return jnp.clip(entries, -most, most).astype(held_as)


def setup_inputs(seed: int = 0, part: int = 0) -> dict:
    arg_keys = jax.random.split(jax.random.key(seed), 8)
    part_splits = jax.random.split(jax.random.fold_in(arg_keys[7], part), 8)
    tokens = normal_values(part_splits[0], (STEPS, TOKENS, D), 1.0, 6.0, ((1, 16),))
    expert_ids_keys = jax.random.split(jax.random.fold_in(part_splits[1], 1), STEPS * TOKENS // TOK_STEP)
    expert_ids_turns = jax.random.permutation(jax.random.fold_in(part_splits[1], 3), STEPS * TOKENS // TOK_STEP)
    expert_ids = jax.vmap(lambda own, number: routed_block(jax.random.fold_in(part_splits[1], 2), own, number, TOK_STEP, EXPERTS, TOPK, CAP, 2))(expert_ids_keys, expert_ids_turns).reshape((STEPS, TOKENS, TOPK))
    gate_weights = jnp.clip(0.19921875 + 0.80078125 * jax.random.uniform(part_splits[2], (STEPS, TOKENS, TOPK), jnp.float32) ** block_scale(part_splits[2], (STEPS, TOKENS, TOPK), ((1, 16),), -0.2, 0.2), 0.19921875, 1.0).astype(jnp.bfloat16)
    w_gate_up = normal_values(arg_keys[3], (D, 2, EXPERTS * FF), D ** -0.5, 0.0625, ((2, 16),))
    w_down = normal_values(arg_keys[4], (EXPERTS * FF, D), FF ** -0.5, 0.125, ((0, 16),))
    shared_gate_up = draw_shared_gate_up(jax.random.fold_in(arg_keys[7], 71), part)
    shared_down = draw_shared_down(jax.random.fold_in(arg_keys[7], 71), part)
    return dict(tokens=tokens, expert_ids=expert_ids, gate_weights=gate_weights, w_gate_up=w_gate_up, w_down=w_down, shared_gate_up=shared_gate_up, shared_down=shared_down)


def reference(tokens, expert_ids, gate_weights, w_gate_up, w_down, shared_gate_up, shared_down):
    group_size = N_FAST // EXPERTS
    slice_size = FF // group_size
    row_total = STEPS * TOKENS
    row_bound = STEPS * N_FAST * CAP
    flat_tokens = jnp.concatenate([tokens.reshape(row_total, D), jnp.zeros((1, D), tokens.dtype)], axis=0)
    flat_ids = expert_ids.reshape(row_total, TOPK)
    flat_gates = gate_weights.reshape(row_total, TOPK).astype(jnp.float32)
    shared_up = shared_gate_up[:, :, :FF].reshape(D, 2 * FF)
    shared_out = shared_down[:FF]
    zero_one = jnp.zeros((1,), jnp.float32)

    def per_expert(accum_rows, expert):
        expert_hit = flat_ids == expert
        chosen = jnp.nonzero(jnp.any(expert_hit, axis=1), size=row_bound, fill_value=row_total)[0].astype(jnp.int32)
        gate_row = jnp.concatenate([jnp.sum(jnp.where(expert_hit, flat_gates, 0.0), axis=1), zero_one])[chosen]
        share_row = jnp.concatenate([expert_hit[:, 0].astype(jnp.float32), zero_one])[chosen]
        picked = flat_tokens[chosen]
        routed_up = lax.dynamic_slice_in_dim(w_gate_up, (expert * FF).astype(jnp.int32), FF, 2).reshape(D, 2 * FF)
        routed_down = lax.dynamic_slice_in_dim(w_down, (expert * FF).astype(jnp.int32), FF, 0)
        routed = jnp.dot(picked, routed_up, preferred_element_type=jnp.float32)
        routed_hidden = (jax.nn.silu(routed[:, :FF]) * routed[:, FF:]).astype(jnp.bfloat16)
        common = jnp.dot(picked, shared_up, preferred_element_type=jnp.float32)
        common_hidden = (jax.nn.silu(common[:, :FF]) * common[:, FF:]).astype(jnp.bfloat16)

        def per_slice(running, slice_index):
            first_unit = (slice_index * slice_size).astype(jnp.int32)
            routed_part = jnp.dot(lax.dynamic_slice_in_dim(routed_hidden, first_unit, slice_size, 1),
                                  lax.dynamic_slice_in_dim(routed_down, first_unit, slice_size, 0),
                                  preferred_element_type=jnp.float32)
            shared_part = jnp.dot(lax.dynamic_slice_in_dim(common_hidden, first_unit, slice_size, 1),
                                  lax.dynamic_slice_in_dim(shared_out, first_unit, slice_size, 0),
                                  preferred_element_type=jnp.float32)
            slice_part = (gate_row[:, None] * routed_part + share_row[:, None] * shared_part).astype(jnp.bfloat16)
            return running + slice_part.astype(jnp.float32), None

        expert_sum, _ = lax.scan(per_slice, jnp.zeros((row_bound, D), jnp.float32),
                                 jnp.arange(group_size, dtype=jnp.int32))
        return accum_rows.at[chosen].add(expert_sum), None

    accum_rows, _ = lax.scan(per_expert, jnp.zeros((row_total + 1, D), jnp.float32),
                             jnp.arange(EXPERTS, dtype=jnp.int32))
    return accum_rows[:row_total].reshape(STEPS, TOKENS, D).astype(jnp.bfloat16)
```

```python
import functools
import math

import jax
import jax.numpy as jnp
from jax import lax
from jax.experimental import pallas as pl
from jax.experimental.pallas import tpu as pltpu
from jax.sharding import PartitionSpec as P

EXPERTS = 8
TOPK = 3
STEPS = 2
CAP = 2
LANES = 128
WIDE = 256
PARTS = 4


def slot_tables(step_tokens, step_ids, step_gates):
    tok_count = step_ids.shape[0]
    flat_ids = step_ids.reshape(tok_count * TOPK)
    expert_hit = (flat_ids[:, None] == jnp.arange(EXPERTS, dtype=jnp.int32)[None, :]).astype(
        jnp.int32
    )
    slot_rank = jnp.sum((jnp.cumsum(expert_hit, axis=0) - expert_hit) * expert_hit, axis=1)
    slot_index = flat_ids * CAP + slot_rank
    placed = (slot_index[:, None] == jnp.arange(EXPERTS * CAP, dtype=jnp.int32)[None, :]).astype(
        jnp.float32
    )
    selector = jnp.sum(placed.reshape(tok_count, TOPK, EXPERTS * CAP), axis=1)
    blocks = jnp.einsum(
        "ts,td->sd", selector.astype(jnp.bfloat16), step_tokens, preferred_element_type=jnp.float32
    ).astype(jnp.bfloat16)
    share_row = jnp.broadcast_to(
        (jnp.arange(TOPK) == 0).astype(jnp.float32)[None, :], (tok_count, TOPK)
    ).reshape(-1)
    gate_row = step_gates.astype(jnp.float32).reshape(-1)
    slot_coefs = jnp.einsum(
        "rs,rc->sc",
        placed,
        jnp.stack([gate_row, share_row], axis=1),
        precision=lax.Precision.HIGHEST,
    ).astype(jnp.bfloat16)
    return (blocks.reshape(EXPERTS, CAP, -1), slot_coefs.reshape(EXPERTS, CAP, 2), selector)


def send_out(blocks, slot_coefs, group_size):
    spread = jnp.repeat(blocks, group_size, axis=0)
    spread_coefs = jnp.repeat(slot_coefs, group_size, axis=0)
    arrived, arrived_coefs = (
        lax.all_to_all(spread, "fast", split_axis=0, concat_axis=0, tiled=True),
        lax.all_to_all(spread_coefs, "fast", split_axis=0, concat_axis=0, tiled=True),
    )
    return (arrived, arrived_coefs)


def expert_work(arrived, arrived_coefs, weights):
    w_gate_up, w_down, shared_gate_up, shared_down = weights
    model_width = arrived.shape[-1]
    hidden_size = w_down.shape[0]
    flat_rows = arrived.reshape(-1, model_width)
    flat_coef = arrived_coefs.reshape(-1, 2).astype(jnp.float32)
    row_count = flat_rows.shape[0]
    block_rows = math.gcd(row_count, 512)
    routed_up = w_gate_up.reshape(model_width, 2 * hidden_size)
    common_up = shared_gate_up.reshape(model_width, 2 * hidden_size)

    def one_block(block_pair):
        row_block, slot_coef = block_pair
        routed = jnp.dot(row_block, routed_up, preferred_element_type=jnp.float32)
        routed_hidden = (jax.nn.silu(routed[:, :hidden_size]) * routed[:, hidden_size:]).astype(
            jnp.bfloat16
        )
        common = jnp.dot(row_block, common_up, preferred_element_type=jnp.float32)
        common_hidden = (jax.nn.silu(common[:, :hidden_size]) * common[:, hidden_size:]).astype(
            jnp.bfloat16
        )
        result = slot_coef[:, 0:1] * jnp.dot(
            routed_hidden, w_down, preferred_element_type=jnp.float32
        )
        result = result + slot_coef[:, 1:2] * jnp.dot(
            common_hidden, shared_down, preferred_element_type=jnp.float32
        )
        return result.astype(jnp.bfloat16)

    outcome = lax.map(
        one_block,
        (flat_rows.reshape(-1, block_rows, model_width), flat_coef.reshape(-1, block_rows, 2)),
    )
    return outcome.reshape(arrived.shape)


def round_trip(blocks, slot_coefs, weights, group_size):
    arrived, arrived_coefs = send_out(blocks, slot_coefs, group_size)
    partials = expert_work(arrived, arrived_coefs, weights)
    returned = lax.all_to_all(partials, "fast", split_axis=0, concat_axis=0, tiled=True)
    slot_count = blocks.shape[1]
    return returned.reshape(EXPERTS, group_size, slot_count, -1).astype(jnp.float32).sum(axis=1)


def finish(selector, summed):
    flat_sums = summed.reshape(selector.shape[1], -1)
    return jnp.dot(
        selector, flat_sums, precision=lax.Precision.HIGHEST, preferred_element_type=jnp.float32
    ).astype(jnp.bfloat16)


def local_exchange(tokens, expert_ids, gate_weights, w_gate_up, w_down, shared_gate_up, shared_down):
    group_size = lax.axis_size("fast") // EXPERTS
    weights = (w_gate_up, w_down, shared_gate_up, shared_down)
    prepared = [
        slot_tables(tokens[step_index], expert_ids[step_index], gate_weights[step_index])
        for step_index in range(STEPS)
    ]
    outputs = []
    model_width = tokens.shape[-1]
    blocks = jnp.stack([member[0] for member in prepared], axis=1).reshape(
        EXPERTS, STEPS * CAP, model_width
    )
    slot_coefs = jnp.stack([member[1] for member in prepared], axis=1).reshape(
        EXPERTS, STEPS * CAP, 2
    )
    summed = round_trip(blocks, slot_coefs, weights, group_size).reshape(
        EXPERTS, STEPS, CAP, model_width
    )
    for step_index in range(STEPS):
        outputs.append(finish(prepared[step_index][2], summed[:, step_index]))
    return jnp.stack(outputs, axis=0)


def fused_kernel(
    n, up_step, down_step,
    tok_ref, wg_ref, wd_ref, sg_ref, sd_ref, out_ref,
    xbuf, wb, wdb, sdb, x2, acc, accs, hid, hids,
    k1, k2, k3, s1, r1, s2, r2, s3, r3,
    wsem, dsem, own_sem, ag_send, ag_recv, c_send, c_recv, x_send, x_recv, z_send, z_recv,
):
    depth, _, units = wg_ref.shape
    rows, wide = tok_ref.shape
    zs = n // 4
    blocks = n
    total = blocks * rows
    tiles = units // LANES
    f = lax.axis_index("fast")
    core, xx, zz = f % 2, (f // 2) % 2, f // 4
    expert = f // (n // EXPERTS)
    core_peer = {"fast": f + 1 - 2 * core}
    x_peer = {"fast": f + 2 - 4 * xx}
    z_of = [(zz + i) % zs for i in range(zs)]

    def z_peer(i):
        return {"fast": z_of[i] * 4 + xx * 2 + core}

    def block_of(c, x, z):
        return c * (2 * zs) + x * zs + z

    flat_g = wg_ref.reshape(2 * depth, units)
    flat_s = sg_ref.reshape(2 * depth, units)
    share_at = pl.multiple_of(expert * LANES, LANES)

    def up_copy(kc, t):
        span = pl.ds(kc * up_step, up_step)
        if t < tiles:
            src = flat_g.at[span, pl.ds(t * LANES, LANES)]
        else:
            src = flat_s.at[span, pl.ds(share_at, LANES)]
        return pltpu.make_async_copy(src, wb.at[t, span], wsem.at[kc, t])

    def down_copies(q):
        cols = pl.ds(q * down_step, down_step)
        return (
            pltpu.make_async_copy(wd_ref.at[:, cols], wdb.at[:, cols], dsem.at[q, 0]),
            pltpu.make_async_copy(
                sd_ref.at[pl.ds(share_at, LANES), cols], sdb.at[:, cols], dsem.at[q, 1]
            ),
        )

    up_chunks = 2 * depth // up_step
    down_chunks = depth // down_step
    for kc in range(up_chunks):
        for t in range(tiles + 1):
            up_copy(kc, t).start()
    for q in range(down_chunks):
        for copy in down_copies(q):
            copy.start()

    barrier = pltpu.get_barrier_semaphore()
    for peer in [core_peer, x_peer] + [z_peer(i) for i in range(1, zs)]:
        pl.semaphore_signal(barrier, inc=1, device_id=peer, device_id_type=pl.DeviceIdType.MESH)
    pl.semaphore_wait(barrier, zs + 1)

    sends = []

    part_cols = depth // PARTS

    def cols_of(p):
        return pl.ds(p * part_cols, part_cols + (LANES if p == PARTS - 1 else 0))

    def send(src, p, block, peer):
        copy = pltpu.make_async_remote_copy(
            src_ref=src,
            dst_ref=xbuf.at[block, :, cols_of(p)],
            send_sem=ag_send.at[len(sends)],
            recv_sem=ag_recv.at[p, block],
            device_id=peer,
            device_id_type=pl.DeviceIdType.MESH,
        )
        copy.start()
        sends.append(copy)

    def arrived(p, block):
        there = xbuf.at[block, :, cols_of(p)]
        pltpu.make_async_copy(tok_ref.at[:, cols_of(p)], there, ag_recv.at[p, block]).wait()
        return there

    mine = block_of(core, xx, zz)
    own = pltpu.make_async_copy(tok_ref, xbuf.at[mine], own_sem)
    own.start()
    for p in range(PARTS):
        for peer in [z_peer(i) for i in range(1, zs)] + [x_peer, core_peer]:
            send(tok_ref.at[:, cols_of(p)], p, mine, peer)

    def pass_z(p):
        for i in range(1, zs):
            block = block_of(core, xx, z_of[i])
            there = arrived(p, block)
            send(there, p, block, x_peer)
            send(there, p, block, core_peer)

    def pass_x(p):
        for i in range(zs):
            block = block_of(core, 1 - xx, z_of[i])
            send(arrived(p, block), p, block, core_peer)

    def settle(p):
        for x in (xx, 1 - xx):
            for i in range(zs):
                arrived(p, block_of(1 - core, x, z_of[i]))

    row_id = lax.broadcasted_iota(jnp.int32, (LANES, 2 * WIDE), 0)
    col_id = lax.broadcasted_iota(jnp.int32, (LANES, 2 * WIDE), 1)
    hit = (col_id == 2 * row_id) | (col_id == WIDE + 2 * row_id + 1)
    spread = jnp.where(hit, 1.0, 0.0).astype(jnp.bfloat16)

    def expand(b, carry):
        at = pl.multiple_of(b * LANES, LANES)
        to = pl.multiple_of(b * WIDE, WIDE)
        part = xbuf[:, :, pl.ds(at, LANES)].astype(jnp.float32).reshape(total, LANES)
        both = jnp.dot(part.astype(jnp.bfloat16), spread, preferred_element_type=jnp.float32)
        x2[0:total, pl.ds(to, WIDE)] = both[:, :WIDE].astype(jnp.bfloat16)
        x2[total : 2 * total, pl.ds(to, WIDE)] = both[:, WIDE:].astype(jnp.bfloat16)
        return carry

    def spread_part(p):
        pieces = part_cols // LANES
        lax.fori_loop(p * pieces, (p + 1) * pieces, expand, 0, unroll=math.gcd(pieces, 7))

    def multiply(kc):
        for t in range(tiles + 1):
            up_copy(kc, t).wait()
        span = pl.ds(kc * up_step, up_step)

        wide = jnp.concatenate([wb[t, span] for t in range(tiles + 1)], axis=1)
        d = jnp.dot(x2[:, span], wide, preferred_element_type=jnp.float32)
        for t in range(tiles // 2):
            if kc == 0:
                acc[t] = d[:, t * WIDE : (t + 1) * WIDE]
            else:
                acc[t] += d[:, t * WIDE : (t + 1) * WIDE]
        if kc == 0:
            accs[...] = d[:, tiles * LANES :]
        else:
            accs[...] += d[:, tiles * LANES :]

    pass_z(0)
    pass_x(0)
    if PARTS > 1:
        pass_z(1)
    settle(0)
    own.wait()
    for p in range(PARTS):
        if p > 0:
            settle(p)
        spread_part(p)
        if p + 1 < PARTS:
            pass_x(p + 1)
        if p + 2 < PARTS:
            pass_z(p + 2)
        for kc in range(p * up_chunks // PARTS, (p + 1) * up_chunks // PARTS):
            multiply(kc)

    table = xbuf[:, :, pl.ds(depth, LANES)].astype(jnp.float32).reshape(total, LANES)
    lane = lax.broadcasted_iota(jnp.int32, (total, LANES), 1)
    gate = jnp.sum(jnp.where(lane == expert, table, 0.0), axis=1, keepdims=True)

    def hidden(both):
        return (jax.nn.silu(both[:total]) * both[total:]).astype(jnp.bfloat16)

    for t in range(tiles // 2):
        hid[:, t * WIDE : (t + 1) * WIDE] = hidden(acc[t])
    hids[...] = hidden(accs[...])

    def remote(src, dst, ssem, rsem, peer):
        return pltpu.make_async_remote_copy(
            src_ref=src, dst_ref=dst, send_sem=ssem, recv_sem=rsem,
            device_id=peer, device_id_type=pl.DeviceIdType.MESH,
        )

    def core_copy(q):
        return remote(s1.at[q], r1.at[q], c_send.at[q], c_recv.at[q], core_peer)

    def x_copy(q):
        return remote(s2.at[q], r2.at[q], x_send.at[q], x_recv.at[q], x_peer)

    def z_copy(q, i):
        return remote(
            s3.at[q, z_of[i]], r3.at[q, zz], z_send.at[q, i], z_recv.at[q, zz], z_peer(i)
        )

    half, quarter = total // 2, total // 4

    def stage_one(q):
        for copy in down_copies(q):
            copy.wait()
        cols = pl.ds(q * down_step, down_step)
        p = gate * jnp.dot(hid[...], wdb[:, cols], preferred_element_type=jnp.float32)
        p = p + jnp.dot(hids[...], sdb[:, cols], preferred_element_type=jnp.float32)
        s1[q] = jnp.where(core == 0, p[half:], p[:half]).astype(jnp.bfloat16)
        core_copy(q).start()
        k1[q % 4] = jnp.where(core == 0, p[:half], p[half:])

    def stage_two(q):
        core_copy(q).wait_recv()
        p = k1[q % 4] + r1[q].astype(jnp.float32)
        s2[q] = jnp.where(xx == 0, p[quarter:], p[:quarter]).astype(jnp.bfloat16)
        x_copy(q).start()
        k2[q % 4] = jnp.where(xx == 0, p[:quarter], p[quarter:])

    def stage_three(q):
        x_copy(q).wait_recv()
        p = (k2[q % 4] + r2[q].astype(jnp.float32)).reshape(zs, rows, down_step)
        s3[q] = p.astype(jnp.bfloat16)
        for i in range(1, zs):
            z_copy(q, i).start()
        keep = jnp.where(zz == 0, p[0], 0.0)
        for z in range(1, zs):
            keep = jnp.where(zz == z, p[z], keep)
        k3[q % 4] = keep

    def stage_four(q):
        p = k3[q % 4]
        for i in range(1, zs):
            slot = r3.at[q, z_of[i]]
            pltpu.make_async_copy(slot, slot, z_recv.at[q, z_of[i]]).wait()
            p = p + r3[q, z_of[i]].astype(jnp.float32)
        out_ref[:, q * down_step : (q + 1) * down_step] = p.astype(jnp.bfloat16)

    for step in range(down_chunks + 7):
        for lag, stage in ((7, stage_four), (4, stage_three), (2, stage_two), (0, stage_one)):
            if 0 <= step - lag < down_chunks:
                stage(step - lag)

    for copy in sends:
        copy.wait_send()
    for q in range(down_chunks):
        core_copy(q).wait_send()
        x_copy(q).wait_send()
        for i in range(1, zs):
            z_copy(q, i).wait_send()


def split_of(size, most):
    best = WIDE
    for step in range(WIDE, most + 1, WIDE):
        if size % step == 0:
            best = step
    return best


def scratch_of(n, rows, depth, units, up_step, down_step):
    total, zs, tiles = n * rows, n // 4, units // LANES
    ups, downs = 2 * depth // up_step, depth // down_step
    bf, fl = jnp.bfloat16, jnp.float32
    buffers = [
        ((n, rows, depth + LANES), bf),
        ((tiles + 1, 2 * depth, LANES), bf),
        ((units, depth), bf),
        ((LANES, depth), bf),
        ((2 * total, 2 * depth), bf),
        ((tiles // 2, 2 * total, WIDE), fl),
        ((2 * total, LANES), fl),
        ((total, units), bf),
        ((total, LANES), bf),
        ((4, total // 2, down_step), fl),
        ((4, total // 4, down_step), fl),
        ((4, rows, down_step), fl),
        ((downs, total // 2, down_step), bf),
        ((downs, total // 2, down_step), bf),
        ((downs, total // 4, down_step), bf),
        ((downs, total // 4, down_step), bf),
        ((downs, zs, rows, down_step), bf),
        ((downs, zs, rows, down_step), bf),
    ]
    dma = pltpu.SemaphoreType.DMA
    sems = [
        dma((ups, tiles + 1)), dma((downs, 2)), dma, dma((PARTS * 4 * zs,)), dma((PARTS, n)),
        dma((downs,)), dma((downs,)), dma((downs,)), dma((downs,)),
        dma((downs, zs)), dma((downs, zs)),
    ]
    size = sum(math.prod(shape) * jnp.dtype(kind).itemsize for shape, kind in buffers)
    return [pltpu.VMEM(shape, kind) for shape, kind in buffers] + sems, size


def local_fused(tokens, expert_ids, gate_weights, w_gate_up, w_down, shared_gate_up, shared_down):
    n = lax.axis_size("fast")
    steps, per_step, depth = tokens.shape
    rows, units = steps * per_step, w_gate_up.shape[2]
    up_step, down_step = split_of(2 * depth // PARTS, 2048), split_of(depth, 1024)
    scratch, _ = scratch_of(n, rows, depth, units, up_step, down_step)
    chosen = expert_ids[..., None] == jnp.arange(LANES, dtype=jnp.int32)
    table = jnp.sum(jnp.where(chosen, gate_weights.astype(jnp.float32)[..., None], 0.0), axis=2)
    sent = jnp.concatenate([tokens, table.astype(jnp.bfloat16)], axis=2).reshape(rows, -1)
    whole = pl.BlockSpec(memory_space=pltpu.VMEM)
    there = pl.BlockSpec(memory_space=pl.ANY)
    out = pl.pallas_call(
        functools.partial(fused_kernel, n, up_step, down_step),
        out_shape=jax.ShapeDtypeStruct((rows, depth), jnp.bfloat16),
        in_specs=[whole, there, there, there, there],
        out_specs=whole,
        scratch_shapes=scratch,
        compiler_params=pltpu.CompilerParams(
            collective_id=0, has_side_effects=True, vmem_limit_bytes=67043328
        ),
    )(sent, w_gate_up, w_down, shared_gate_up, shared_down)
    return out.reshape(steps, per_step, depth)


def local(tokens, expert_ids, gate_weights, w_gate_up, w_down, shared_gate_up, shared_down):
    n = lax.axis_size("fast")
    steps, per_step, depth = tokens.shape
    rows, units = steps * per_step, w_gate_up.shape[2]
    fits = n % 8 == 0 and rows % 8 == 0 and units == EXPERTS * LANES and depth % (PARTS * LANES) == 0
    if fits:
        sizes = (n, rows, depth, units, split_of(2 * depth // PARTS, 2048), split_of(depth, 1024))
        fits = scratch_of(*sizes)[1] < 66 * 10**6
    run = local_fused if fits else local_exchange
    return run(
        tokens, expert_ids, gate_weights, w_gate_up, w_down, shared_gate_up, shared_down
    )


def solution(mesh):
    placed = (
        P(None, ("rep", "fast"), None),
        P(None, ("rep", "fast"), None),
        P(None, ("rep", "fast"), None),
        P(None, None, "fast"),
        P("fast", None),
        P(None, None, "fast"),
        P("fast", None),
    )
    return jax.shard_map(
        local, mesh=mesh, in_specs=placed, out_specs=P(None, ("rep", "fast"), None), check_vma=False
    )
```

```python
import functools
import math

import jax
import jax.numpy as jnp
from jax import lax
from jax.experimental import pallas as pl
from jax.experimental.pallas import tpu as pltpu
from jax.sharding import PartitionSpec as P

EXPERTS = 8
TOPK = 3
STEPS = 2
CAP = 2
LANES = 128
WIDE = 256
PARTS = 4
DOWNS = 7
KEPT = 4


def slot_tables(step_tokens, step_ids, step_gates):
    tok_count = step_ids.shape[0]
    flat_ids = step_ids.reshape(tok_count * TOPK)
    expert_hit = (flat_ids[:, None] == jnp.arange(EXPERTS, dtype=jnp.int32)[None, :]).astype(
        jnp.int32
    )
    slot_rank = jnp.sum((jnp.cumsum(expert_hit, axis=0) - expert_hit) * expert_hit, axis=1)
    slot_index = flat_ids * CAP + slot_rank
    placed = (slot_index[:, None] == jnp.arange(EXPERTS * CAP, dtype=jnp.int32)[None, :]).astype(
        jnp.float32
    )
    selector = jnp.sum(placed.reshape(tok_count, TOPK, EXPERTS * CAP), axis=1)
    blocks = jnp.einsum(
        "ts,td->sd", selector.astype(jnp.bfloat16), step_tokens, preferred_element_type=jnp.float32
    ).astype(jnp.bfloat16)
    share_row = jnp.broadcast_to(
        (jnp.arange(TOPK) == 0).astype(jnp.float32)[None, :], (tok_count, TOPK)
    ).reshape(-1)
    gate_row = step_gates.astype(jnp.float32).reshape(-1)
    slot_coefs = jnp.einsum(
        "rs,rc->sc",
        placed,
        jnp.stack([gate_row, share_row], axis=1),
        precision=lax.Precision.HIGHEST,
    ).astype(jnp.bfloat16)
    return (blocks.reshape(EXPERTS, CAP, -1), slot_coefs.reshape(EXPERTS, CAP, 2), selector)


def send_out(blocks, slot_coefs, group_size):
    spread = jnp.repeat(blocks, group_size, axis=0)
    spread_coefs = jnp.repeat(slot_coefs, group_size, axis=0)
    arrived, arrived_coefs = (
        lax.all_to_all(spread, "fast", split_axis=0, concat_axis=0, tiled=True),
        lax.all_to_all(spread_coefs, "fast", split_axis=0, concat_axis=0, tiled=True),
    )
    return (arrived, arrived_coefs)


def expert_work(arrived, arrived_coefs, weights):
    w_gate_up, w_down, shared_gate_up, shared_down = weights
    model_width = arrived.shape[-1]
    hidden_size = w_down.shape[0]
    flat_rows = arrived.reshape(-1, model_width)
    flat_coef = arrived_coefs.reshape(-1, 2).astype(jnp.float32)
    row_count = flat_rows.shape[0]
    block_rows = math.gcd(row_count, 512)
    routed_up = w_gate_up.reshape(model_width, 2 * hidden_size)
    common_up = shared_gate_up.reshape(model_width, 2 * hidden_size)

    def one_block(block_pair):
        row_block, slot_coef = block_pair
        routed = jnp.dot(row_block, routed_up, preferred_element_type=jnp.float32)
        routed_hidden = (jax.nn.silu(routed[:, :hidden_size]) * routed[:, hidden_size:]).astype(
            jnp.bfloat16
        )
        common = jnp.dot(row_block, common_up, preferred_element_type=jnp.float32)
        common_hidden = (jax.nn.silu(common[:, :hidden_size]) * common[:, hidden_size:]).astype(
            jnp.bfloat16
        )
        result = slot_coef[:, 0:1] * jnp.dot(
            routed_hidden, w_down, preferred_element_type=jnp.float32
        )
        result = result + slot_coef[:, 1:2] * jnp.dot(
            common_hidden, shared_down, preferred_element_type=jnp.float32
        )
        return result.astype(jnp.bfloat16)

    outcome = lax.map(
        one_block,
        (flat_rows.reshape(-1, block_rows, model_width), flat_coef.reshape(-1, block_rows, 2)),
    )
    return outcome.reshape(arrived.shape)


def round_trip(blocks, slot_coefs, weights, group_size):
    arrived, arrived_coefs = send_out(blocks, slot_coefs, group_size)
    partials = expert_work(arrived, arrived_coefs, weights)
    returned = lax.all_to_all(partials, "fast", split_axis=0, concat_axis=0, tiled=True)
    slot_count = blocks.shape[1]
    return returned.reshape(EXPERTS, group_size, slot_count, -1).astype(jnp.float32).sum(axis=1)


def finish(selector, summed):
    flat_sums = summed.reshape(selector.shape[1], -1)
    return jnp.dot(
        selector, flat_sums, precision=lax.Precision.HIGHEST, preferred_element_type=jnp.float32
    ).astype(jnp.bfloat16)


def local_exchange(tokens, expert_ids, gate_weights, w_gate_up, w_down, shared_gate_up, shared_down):
    group_size = lax.axis_size("fast") // EXPERTS
    weights = (w_gate_up, w_down, shared_gate_up, shared_down)
    prepared = [
        slot_tables(tokens[step_index], expert_ids[step_index], gate_weights[step_index])
        for step_index in range(STEPS)
    ]
    outputs = []
    model_width = tokens.shape[-1]
    blocks = jnp.stack([member[0] for member in prepared], axis=1).reshape(
        EXPERTS, STEPS * CAP, model_width
    )
    slot_coefs = jnp.stack([member[1] for member in prepared], axis=1).reshape(
        EXPERTS, STEPS * CAP, 2
    )
    summed = round_trip(blocks, slot_coefs, weights, group_size).reshape(
        EXPERTS, STEPS, CAP, model_width
    )
    for step_index in range(STEPS):
        outputs.append(finish(prepared[step_index][2], summed[:, step_index]))
    return jnp.stack(outputs, axis=0)


def fused_kernel(
    n,
    tok_ref, ids_ref, gates_ref, wg_ref, wd_ref, sg_ref, sd_ref, out_ref,
    wb, wsb, x2, x2s, acc, accs, hid, hids, pick, mix,
    dsp, xr, xs, k1, s1, r1, s2, r2,
    up_sem, down_sem, d_send, d_recv, f_send, f_recv, sx_send, sx_recv, sc_send, sc_recv,
    c_send, c_recv, z_send, z_recv, x_send, x_recv,
):
    depth, _, units = wg_ref.shape
    steps, per_step, _ = tok_ref.shape
    rows = steps * per_step
    zs, chips = n // 4, n // 2
    slots = chips * rows
    tiles, share_tiles = units // LANES, units // (2 * LANES)
    share = share_tiles * LANES
    part, half = depth // PARTS, depth // PARTS // 2
    down, wide = depth // DOWNS, depth // DOWNS // 2
    f = lax.axis_index("fast")
    core, xx, zz = f % 2, (f // 2) % 2, f // 4
    me = f // 2
    core_peer = {"fast": f + 1 - 2 * core}
    x_peer = {"fast": f + 2 - 4 * xx}
    away = [(dz, dx) for dz in range(1, zs) for dx in (0, 1)] + [(0, 1)]

    def chip_of(i):
        dz, dx = away[i]
        return ((zz + dz) % zs) * 2 + (xx + dx) % 2

    def peer_of(i):
        return {"fast": chip_of(i) * 2 + core}

    def remote(src, dst, ssem, rsem, peer):
        return pltpu.make_async_remote_copy(
            src_ref=src, dst_ref=dst, send_sem=ssem, recv_sem=rsem,
            device_id=peer, device_id_type=pl.DeviceIdType.MESH,
        )

    flat_g = wg_ref.reshape(2 * depth, units)
    flat_s = sg_ref.reshape(2 * depth, units)
    share_at = pl.multiple_of(xx * share, share)

    def up_copies(p):
        span = pl.ds(2 * p * part, 2 * part)
        for t in range(tiles):
            yield pltpu.make_async_copy(
                flat_g.at[span, pl.ds(t * LANES, LANES)], wb.at[t, span], up_sem.at[p, t]
            )
        for t in range(share_tiles):
            yield pltpu.make_async_copy(
                flat_s.at[span, pl.ds(share_at + t * LANES, LANES)],
                wsb.at[t, span],
                up_sem.at[p, tiles + t],
            )

    def down_place(c):
        return wb.at[c % tiles, pl.ds((c // tiles) * units, units)]

    def share_place(c):
        return wsb.at[c % share_tiles, pl.ds((c // share_tiles) * share, share)]

    down_tiles = down // LANES

    def down_copies(q):
        for i in range(down_tiles):
            c = q * down_tiles + i
            cols = pl.ds(c * LANES, LANES)
            yield pltpu.make_async_copy(wd_ref.at[:, cols], down_place(c), down_sem.at[q, i])
            yield pltpu.make_async_copy(
                sd_ref.at[pl.ds(share_at, share), cols],
                share_place(c),
                down_sem.at[q, down_tiles + i],
            )

    def start(copies):
        for copy in copies:
            copy.start()

    for p in range(PARTS):
        start(up_copies(p))

    barrier = pltpu.get_barrier_semaphore()
    for peer in [core_peer] + [peer_of(i) for i in range(len(away))]:
        pl.semaphore_signal(barrier, inc=1, device_id=peer, device_id_type=pl.DeviceIdType.MESH)

    slot = lax.broadcasted_iota(jnp.int32, (slots, 2 * rows), 0)
    lane = lax.broadcasted_iota(jnp.int32, (slots, 2 * rows), 1)
    slot_expert, slot_step, slot_cap = slot // rows, slot % (rows // 2) // CAP, slot % CAP
    lane_step = lane % rows // per_step
    named = jnp.zeros((slots, 2 * rows), jnp.float32)
    gate = jnp.zeros((slots, 2 * rows), jnp.float32)
    for k in range(TOPK):
        ids = jnp.concatenate([ids_ref[k, s : s + 1, :] for s in range(steps)] * 2, axis=1)
        gates = gates_ref[k].astype(jnp.float32)
        gates = jnp.concatenate([gates[s : s + 1, :] for s in range(steps)] * 2, axis=1)
        match = ids == slot_expert
        named = named + jnp.where(match, 1.0, 0.0)
        gate = gate + jnp.where(match, gates, 0.0)
    before = lax.broadcasted_iota(jnp.int32, (2 * rows, 2 * rows), 0)
    after = lax.broadcasted_iota(jnp.int32, (2 * rows, 2 * rows), 1)
    earlier = jnp.where((before // per_step == after // per_step) & (before < after), 1.0, 0.0)
    rank = jnp.dot(
        named.astype(jnp.bfloat16), earlier.astype(jnp.bfloat16), preferred_element_type=jnp.float32
    )
    here = (rank == slot_cap.astype(jnp.float32)) & (lane_step == slot_step)
    placed = jnp.where(here, named, 0.0)
    gate = jnp.where(here, gate, 0.0)
    low = slot % rows < rows // 2
    weight = jnp.where((lane < rows) == low, gate, 0.0)
    eye_r = lax.broadcasted_iota(jnp.int32, (slots, slots), 0)
    eye_c = lax.broadcasted_iota(jnp.int32, (slots, slots), 1)
    eye = jnp.where(eye_r == eye_c, 1.0, 0.0).astype(jnp.bfloat16)
    mix[...] = lax.dot_general(
        weight.astype(jnp.bfloat16), eye, (((0,), (0,)), ((), ())), preferred_element_type=jnp.float32
    ).astype(jnp.bfloat16)
    own_r = lax.broadcasted_iota(jnp.int32, (rows, rows), 0)
    own_c = lax.broadcasted_iota(jnp.int32, (rows, rows), 1)
    pick[0:slots] = placed[:, :rows]
    pick[slots : slots + rows] = jnp.where(own_r == own_c, 1.0, 0.0)

    upper = lax.broadcasted_iota(jnp.int32, (slots, half), 0) % rows < rows // 2

    def lay_out(p):
        chooser = pick[...].astype(jnp.bfloat16)
        x = jnp.concatenate(
            [tok_ref[s, :, p * part : (p + 1) * part].astype(jnp.float32) for s in range(steps)], axis=0
        ).astype(jnp.bfloat16)
        a = jnp.dot(chooser, x[:, :half], preferred_element_type=jnp.float32)
        b = jnp.dot(chooser, x[:, half:], preferred_element_type=jnp.float32)
        block = jnp.where(upper, a[:slots], b[:slots]).reshape(chips, rows, half)
        dsp[p] = block.astype(jnp.bfloat16)
        xs[p, core, xx, :, 0:half] = a[slots:].astype(jnp.bfloat16)
        xs[p, core, xx, :, half:part] = b[slots:].astype(jnp.bfloat16)
        xr[p, core, me] = dsp[p, me]

    def slot_send(p, i):
        return remote(
            dsp.at[p, chip_of(i)], xr.at[p, core, me], d_send.at[p, i], d_recv.at[p, me], peer_of(i)
        )

    def share_send(p):
        return remote(
            xs.at[p, core, xx], xs.at[p, core, xx], sx_send.at[p], sx_recv.at[p], x_peer
        )

    def slot_pass(p):
        return remote(xr.at[p, core], xr.at[p, core], f_send.at[p], f_recv.at[p], core_peer)

    def share_pass(p):
        return remote(xs.at[p, core], xs.at[p, core], sc_send.at[p], sc_recv.at[p], core_peer)

    for p in range(PARTS):
        lay_out(p)
        if p == 0:
            pl.semaphore_wait(barrier, len(away) + 1)
        for i in range(len(away)):
            slot_send(p, i).start()
        share_send(p).start()

    def landed(ref, sem):
        pltpu.make_async_copy(ref, ref, sem).wait()

    def forward(p):
        landed(xs.at[p, core, 1 - xx], sx_recv.at[p])
        share_pass(p).start()
        for i in range(len(away)):
            landed(xr.at[p, core, chip_of(i)], d_recv.at[p, chip_of(i)])
        slot_pass(p).start()

    def settle(p):
        landed(xs.at[p, 1 - core], sc_recv.at[p])
        landed(xr.at[p, 1 - core], f_recv.at[p])

    row_id = lax.broadcasted_iota(jnp.int32, (LANES, 2 * WIDE), 0)
    col_id = lax.broadcasted_iota(jnp.int32, (LANES, 2 * WIDE), 1)
    hit = (col_id == 2 * row_id) | (col_id == WIDE + 2 * row_id + 1)
    spread = jnp.where(hit, 1.0, 0.0).astype(jnp.bfloat16)
    first = lax.broadcasted_iota(jnp.int32, (slots, LANES), 0) % rows < rows // 2
    shared_rows = 4 * rows

    def expand(p):
        for j in range(half // LANES):
            cols = slice(j * LANES, (j + 1) * LANES)
            b0 = xr[p, 0, :, :, cols].astype(jnp.float32).reshape(slots, LANES)
            b1 = xr[p, 1, :, :, cols].astype(jnp.float32).reshape(slots, LANES)
            pieces = [
                jnp.where(first, b0, pltpu.roll(b1, rows // 2, 0)),
                jnp.where(first, pltpu.roll(b0, slots - rows // 2, 0), b1),
            ]
            for h in range(2):
                at = h * half + j * LANES
                piece = xs[p, :, :, :, at : at + LANES].astype(jnp.float32)
                pieces.append(piece.reshape(shared_rows, LANES))
            mixed = jnp.concatenate(pieces, axis=0).astype(jnp.bfloat16)
            both = jnp.dot(mixed, spread, preferred_element_type=jnp.float32).astype(jnp.bfloat16)
            for h in range(2):
                to = 2 * (p * part + h * half + j * LANES)
                for g in range(2):
                    ways = slice(g * WIDE, (g + 1) * WIDE)
                    x2[g * slots : (g + 1) * slots, to : to + WIDE] = both[
                        h * slots : (h + 1) * slots, ways
                    ]
                    x2s[g * shared_rows : (g + 1) * shared_rows, to : to + WIDE] = both[
                        2 * slots + h * shared_rows : 2 * slots + (h + 1) * shared_rows, ways
                    ]

    def multiply(p):
        for copy in up_copies(p):
            copy.wait()
        span = pl.ds(2 * p * part, 2 * part)
        w = jnp.concatenate([wb[t, span] for t in range(tiles)], axis=1)
        d = jnp.dot(x2[:, span], w, preferred_element_type=jnp.float32)
        w = jnp.concatenate([wsb[t, span] for t in range(share_tiles)], axis=1)
        ds = jnp.dot(x2s[:, span], w, preferred_element_type=jnp.float32)
        if p == 0:
            acc[...] = d
            accs[...] = ds
        else:
            acc[...] += d
            accs[...] += ds

    free_after = [
        next(
            p for p in range(PARTS)
            if max(
                ((q + 1) * down_tiles + tiles - 1) // tiles * units,
                ((q + 1) * down_tiles + share_tiles - 1) // share_tiles * share,
            ) <= 2 * part * (p + 1)
        )
        for q in range(DOWNS)
    ]
    for p in range(PARTS):
        forward(p)
        settle(p)
        expand(p)
        multiply(p)
        for q in range(DOWNS):
            if max(free_after[q], 1) == p:
                start(down_copies(q))

    def hidden(both, m):
        return (jax.nn.silu(both[:m]) * both[m:]).astype(jnp.bfloat16)

    hid[...] = hidden(acc[...], slots)
    hids[...] = hidden(accs[...], shared_rows)

    def core_copy(q):
        return remote(s1.at[q], r1.at[q], c_send.at[q], c_recv.at[q], core_peer)

    def slot_copy(q, i):
        return remote(
            s2.at[q, chip_of(i)], r2.at[q, me], z_send.at[q, i], z_recv.at[q, me], peer_of(i)
        )

    def x_copy(q):
        return remote(
            s2.at[q, pl.ds(chips + 2 * (1 - xx), 2)],
            r2.at[q, pl.ds(chips, 2)],
            x_send.at[q],
            x_recv.at[q],
            x_peer,
        )

    top = lax.broadcasted_iota(jnp.int32, (slots, wide), 0) % rows < rows // 2
    mine = 2 * rows

    def stage_one(q):
        for copy in down_copies(q):
            copy.wait()
        cs = range(q * down_tiles, (q + 1) * down_tiles)
        w = jnp.concatenate([down_place(c)[...] for c in cs], axis=1)
        a = jnp.dot(hid[...], w, preferred_element_type=jnp.float32)
        w = jnp.concatenate([share_place(c)[...] for c in cs], axis=1)
        b = jnp.dot(hids[...], w, preferred_element_type=jnp.float32)
        lo, hi = a[:, :wide], a[:, wide:]
        t0 = jnp.where(top, lo, pltpu.roll(hi, rows // 2, 0))
        t1 = jnp.where(top, pltpu.roll(lo, slots - rows // 2, 0), hi)

        def pack(t, u):
            return jnp.concatenate(
                [t, u[:rows, :wide], u[:rows, wide:], u[rows:, :wide], u[rows:, wide:]], axis=0
            )

        p0, p1 = pack(t0, b[:mine]), pack(t1, b[mine:])
        s1[q] = jnp.where(core == 0, p1, p0).astype(jnp.bfloat16)
        core_copy(q).start()
        k1[q % KEPT] = jnp.where(core == 0, p0, p1)

    def stage_two(q):
        core_copy(q).wait_recv()
        p = k1[q % KEPT] + r1[q].astype(jnp.float32)
        s2[q] = p.reshape(chips + 4, rows, wide).astype(jnp.bfloat16)
        for i in range(len(away)):
            slot_copy(q, i).start()
        x_copy(q).start()
        r2[q, me] = s2[q, me]

    def stage_three(q):
        for i in range(len(away)):
            landed(r2.at[q, chip_of(i)], z_recv.at[q, chip_of(i)])
        x_copy(q).wait_recv()
        back = r2[q, 0:chips].astype(jnp.float32).reshape(slots, wide).astype(jnp.bfloat16)
        both = jnp.dot(mix[...], back, preferred_element_type=jnp.float32)
        for h in range(2):
            p = both[h * rows : (h + 1) * rows]
            p = p + r2[q, chips + h].astype(jnp.float32)
            p = p + s2[q, chips + 2 * xx + h].astype(jnp.float32)
            p = p.astype(jnp.bfloat16).astype(jnp.float32)
            at = q * down + h * wide
            for s in range(steps):
                out_ref[s, :, at : at + wide] = p[s * per_step : (s + 1) * per_step].astype(
                    jnp.bfloat16
                )

    for step in range(DOWNS + 2):
        if step >= 2:
            stage_two(step - 2)
        if step < DOWNS:
            stage_one(step)
    for q in range(DOWNS):
        stage_three(q)

    for p in range(PARTS):
        for i in range(len(away)):
            slot_send(p, i).wait_send()
        for copy in (share_send(p), slot_pass(p), share_pass(p)):
            copy.wait_send()
    for q in range(DOWNS):
        core_copy(q).wait_send()
        x_copy(q).wait_send()
        for i in range(len(away)):
            slot_copy(q, i).wait_send()


def scratch_of(n, rows, depth, units):
    chips = n // 2
    slots, shared = chips * rows, 4 * rows
    tiles, share_tiles = units // LANES, units // (2 * LANES)
    part, half = depth // PARTS, depth // PARTS // 2
    wide, down_tiles = depth // DOWNS // 2, depth // DOWNS // LANES
    bf, fl = jnp.bfloat16, jnp.float32
    packed = slots + 4 * rows
    buffers = [
        ((tiles, 2 * depth, LANES), bf),
        ((share_tiles, 2 * depth, LANES), bf),
        ((2 * slots, 2 * depth), bf),
        ((2 * shared, 2 * depth), bf),
        ((2 * slots, units), fl),
        ((2 * shared, share_tiles * LANES), fl),
        ((slots, units), bf),
        ((shared, share_tiles * LANES), bf),
        ((slots + rows, rows), fl),
        ((2 * rows, slots), bf),
        ((PARTS, chips, rows, half), bf),
        ((PARTS, 2, chips, rows, half), bf),
        ((PARTS, 2, 2, rows, part), bf),
        ((KEPT, packed, wide), fl),
        ((DOWNS, packed, wide), bf),
        ((DOWNS, packed, wide), bf),
        ((DOWNS, chips + 4, rows, wide), bf),
        ((DOWNS, chips + 2, rows, wide), bf),
    ]
    dma = pltpu.SemaphoreType.DMA
    sems = [
        dma((PARTS, tiles + share_tiles)), dma((DOWNS, 2 * down_tiles)),
        dma((PARTS, chips)), dma((PARTS, chips)),
        dma((PARTS,)), dma((PARTS,)), dma((PARTS,)), dma((PARTS,)), dma((PARTS,)), dma((PARTS,)),
        dma((DOWNS,)), dma((DOWNS,)), dma((DOWNS, chips)), dma((DOWNS, chips)),
        dma((DOWNS,)), dma((DOWNS,)),
    ]
    return [pltpu.VMEM(shape, kind) for shape, kind in buffers] + sems


def local_fused(tokens, expert_ids, gate_weights, w_gate_up, w_down, shared_gate_up, shared_down):
    n = lax.axis_size("fast")
    steps, per_step, depth = tokens.shape
    rows, units = steps * per_step, w_gate_up.shape[2]
    whole = pl.BlockSpec(memory_space=pltpu.VMEM)
    there = pl.BlockSpec(memory_space=pl.ANY)
    return pl.pallas_call(
        functools.partial(fused_kernel, n),
        out_shape=jax.ShapeDtypeStruct((steps, per_step, depth), jnp.bfloat16),
        in_specs=[whole, whole, whole, there, there, there, there],
        out_specs=whole,
        scratch_shapes=scratch_of(n, rows, depth, units),
        compiler_params=pltpu.CompilerParams(
            collective_id=0, has_side_effects=True, vmem_limit_bytes=67043328
        ),
    )(
        tokens,
        jnp.transpose(expert_ids, (2, 0, 1)),
        jnp.transpose(gate_weights, (2, 0, 1)),
        w_gate_up, w_down, shared_gate_up, shared_down,
    )


def local(tokens, expert_ids, gate_weights, w_gate_up, w_down, shared_gate_up, shared_down):
    n = lax.axis_size("fast")
    steps, per_step, depth = tokens.shape
    units = w_gate_up.shape[2]
    fits = n == 2 * EXPERTS and steps == STEPS and per_step == 2 * CAP
    fits = fits and units == EXPERTS * LANES and depth == 7 * EXPERTS * LANES
    run = local_fused if fits else local_exchange
    return run(
        tokens, expert_ids, gate_weights, w_gate_up, w_down, shared_gate_up, shared_down
    )


def solution(mesh):
    placed = (
        P(None, ("rep", "fast"), None),
        P(None, ("rep", "fast"), None),
        P(None, ("rep", "fast"), None),
        P(None, None, "fast"),
        P("fast", None),
        P(None, None, "fast"),
        P("fast", None),
    )
    return jax.shard_map(
        local, mesh=mesh, in_specs=placed, out_specs=P(None, ("rep", "fast"), None), check_vma=False
    )
```

```python
import functools
import math

import jax
import jax.numpy as jnp
from jax import lax
from jax.experimental import pallas as pl
from jax.experimental.pallas import tpu as pltpu
from jax.sharding import PartitionSpec as P

EXPERTS = 8
TOPK = 3
STEPS = 2
CAP = 2
LANES = 128
WIDE = 256
PART_UNITS = (7, 7, 7, 7)
DOWN_UNITS = (7, 7, 7, 7)
PARTS = len(PART_UNITS)
DOWNS = len(DOWN_UNITS)


def slot_tables(step_tokens, step_ids, step_gates):
    tok_count = step_ids.shape[0]
    flat_ids = step_ids.reshape(tok_count * TOPK)
    expert_hit = (flat_ids[:, None] == jnp.arange(EXPERTS, dtype=jnp.int32)[None, :]).astype(
        jnp.int32
    )
    slot_rank = jnp.sum((jnp.cumsum(expert_hit, axis=0) - expert_hit) * expert_hit, axis=1)
    slot_index = flat_ids * CAP + slot_rank
    placed = (slot_index[:, None] == jnp.arange(EXPERTS * CAP, dtype=jnp.int32)[None, :]).astype(
        jnp.float32
    )
    selector = jnp.sum(placed.reshape(tok_count, TOPK, EXPERTS * CAP), axis=1)
    blocks = jnp.einsum(
        "ts,td->sd", selector.astype(jnp.bfloat16), step_tokens, preferred_element_type=jnp.float32
    ).astype(jnp.bfloat16)
    share_row = jnp.broadcast_to(
        (jnp.arange(TOPK) == 0).astype(jnp.float32)[None, :], (tok_count, TOPK)
    ).reshape(-1)
    gate_row = step_gates.astype(jnp.float32).reshape(-1)
    slot_coefs = jnp.einsum(
        "rs,rc->sc",
        placed,
        jnp.stack([gate_row, share_row], axis=1),
        precision=lax.Precision.HIGHEST,
    ).astype(jnp.bfloat16)
    return (blocks.reshape(EXPERTS, CAP, -1), slot_coefs.reshape(EXPERTS, CAP, 2), selector)


def send_out(blocks, slot_coefs, group_size):
    spread = jnp.repeat(blocks, group_size, axis=0)
    spread_coefs = jnp.repeat(slot_coefs, group_size, axis=0)
    arrived, arrived_coefs = (
        lax.all_to_all(spread, "fast", split_axis=0, concat_axis=0, tiled=True),
        lax.all_to_all(spread_coefs, "fast", split_axis=0, concat_axis=0, tiled=True),
    )
    return (arrived, arrived_coefs)


def expert_work(arrived, arrived_coefs, weights):
    w_gate_up, w_down, shared_gate_up, shared_down = weights
    model_width = arrived.shape[-1]
    hidden_size = w_down.shape[0]
    flat_rows = arrived.reshape(-1, model_width)
    flat_coef = arrived_coefs.reshape(-1, 2).astype(jnp.float32)
    row_count = flat_rows.shape[0]
    block_rows = math.gcd(row_count, 512)
    routed_up = w_gate_up.reshape(model_width, 2 * hidden_size)
    common_up = shared_gate_up.reshape(model_width, 2 * hidden_size)

    def one_block(block_pair):
        row_block, slot_coef = block_pair
        routed = jnp.dot(row_block, routed_up, preferred_element_type=jnp.float32)
        routed_hidden = (jax.nn.silu(routed[:, :hidden_size]) * routed[:, hidden_size:]).astype(
            jnp.bfloat16
        )
        common = jnp.dot(row_block, common_up, preferred_element_type=jnp.float32)
        common_hidden = (jax.nn.silu(common[:, :hidden_size]) * common[:, hidden_size:]).astype(
            jnp.bfloat16
        )
        result = slot_coef[:, 0:1] * jnp.dot(
            routed_hidden, w_down, preferred_element_type=jnp.float32
        )
        result = result + slot_coef[:, 1:2] * jnp.dot(
            common_hidden, shared_down, preferred_element_type=jnp.float32
        )
        return result.astype(jnp.bfloat16)

    outcome = lax.map(
        one_block,
        (flat_rows.reshape(-1, block_rows, model_width), flat_coef.reshape(-1, block_rows, 2)),
    )
    return outcome.reshape(arrived.shape)


def round_trip(blocks, slot_coefs, weights, group_size):
    arrived, arrived_coefs = send_out(blocks, slot_coefs, group_size)
    partials = expert_work(arrived, arrived_coefs, weights)
    returned = lax.all_to_all(partials, "fast", split_axis=0, concat_axis=0, tiled=True)
    slot_count = blocks.shape[1]
    return returned.reshape(EXPERTS, group_size, slot_count, -1).astype(jnp.float32).sum(axis=1)


def finish(selector, summed):
    flat_sums = summed.reshape(selector.shape[1], -1)
    return jnp.dot(
        selector, flat_sums, precision=lax.Precision.HIGHEST, preferred_element_type=jnp.float32
    ).astype(jnp.bfloat16)


def local_exchange(tokens, expert_ids, gate_weights, w_gate_up, w_down, shared_gate_up, shared_down):
    group_size = lax.axis_size("fast") // EXPERTS
    weights = (w_gate_up, w_down, shared_gate_up, shared_down)
    prepared = [
        slot_tables(tokens[step_index], expert_ids[step_index], gate_weights[step_index])
        for step_index in range(STEPS)
    ]
    outputs = []
    model_width = tokens.shape[-1]
    blocks = jnp.stack([member[0] for member in prepared], axis=1).reshape(
        EXPERTS, STEPS * CAP, model_width
    )
    slot_coefs = jnp.stack([member[1] for member in prepared], axis=1).reshape(
        EXPERTS, STEPS * CAP, 2
    )
    summed = round_trip(blocks, slot_coefs, weights, group_size).reshape(
        EXPERTS, STEPS, CAP, model_width
    )
    for step_index in range(STEPS):
        outputs.append(finish(prepared[step_index][2], summed[:, step_index]))
    return jnp.stack(outputs, axis=0)


def spans(size, units):
    unit = size // sum(units)
    return [(unit * sum(units[:i]), unit * count) for i, count in enumerate(units)]


def fused_kernel(
    n,
    tok_ref, ids_ref, gates_ref, wg_ref, wd_ref, sg_ref, sd_ref, out_ref,
    wb, wsb, x2, x2s, acc, accs, hid, hids, pick, mix,
    dsp, xr, xs, k1, s1, r1, s2, r2,
    up_sem, down_sem, d_send, d_recv, f_send, f_recv, sx_send, sx_recv, sc_send, sc_recv,
    c_send, c_recv, z_send, z_recv, x_send, x_recv,
):
    depth, _, units = wg_ref.shape
    steps, per_step, _ = tok_ref.shape
    rows = steps * per_step
    zs, chips = n // 4, n // 2
    slots = chips * rows
    tiles, share_tiles = units // LANES, units // (2 * LANES)
    share = share_tiles * LANES
    parts, downs = spans(depth, PART_UNITS), spans(depth, DOWN_UNITS)
    f = lax.axis_index("fast")
    core, xx, zz = f % 2, (f // 2) % 2, f // 4
    me = f // 2
    core_peer = {"fast": f + 1 - 2 * core}
    x_peer = {"fast": f + 2 - 4 * xx}
    away = [(dz, dx) for dz in range(1, zs) for dx in (0, 1)] + [(0, 1)]

    def chip_of(i):
        dz, dx = away[i]
        return ((zz + dz) % zs) * 2 + (xx + dx) % 2

    def peer_of(i):
        return {"fast": chip_of(i) * 2 + core}

    def remote(src, dst, ssem, rsem, peer):
        return pltpu.make_async_remote_copy(
            src_ref=src, dst_ref=dst, send_sem=ssem, recv_sem=rsem,
            device_id=peer, device_id_type=pl.DeviceIdType.MESH,
        )

    barrier = pltpu.get_barrier_semaphore()
    for peer in [core_peer] + [peer_of(i) for i in range(len(away))]:
        pl.semaphore_signal(barrier, inc=1, device_id=peer, device_id_type=pl.DeviceIdType.MESH)

    flat_g = wg_ref.reshape(2 * depth, units)
    flat_s = sg_ref.reshape(2 * depth, units)
    share_at = pl.multiple_of(xx * share, share)

    def up_copies(p):
        span = pl.ds(2 * parts[p][0], 2 * parts[p][1])
        for t in range(tiles):
            yield pltpu.make_async_copy(
                flat_g.at[span, pl.ds(t * LANES, LANES)], wb.at[t, span], up_sem.at[p, t]
            )
        for t in range(share_tiles):
            yield pltpu.make_async_copy(
                flat_s.at[span, pl.ds(share_at + t * LANES, LANES)],
                wsb.at[t, span],
                up_sem.at[p, tiles + t],
            )

    def down_place(c):
        return wb.at[c % tiles, pl.ds((c // tiles) * units, units)]

    def share_place(c):
        return wsb.at[c % share_tiles, pl.ds((c // share_tiles) * share, share)]

    def down_range(q):
        at, size = downs[q]
        return range(at // LANES, (at + size) // LANES)

    def down_copies(q):
        for i, c in enumerate(down_range(q)):
            cols = pl.ds(c * LANES, LANES)
            yield pltpu.make_async_copy(wd_ref.at[:, cols], down_place(c), down_sem.at[q, i])
            yield pltpu.make_async_copy(
                sd_ref.at[pl.ds(share_at, share), cols],
                share_place(c),
                down_sem.at[q, len(down_range(q)) + i],
            )

    def begin(copies):
        for copy in copies:
            copy.start()

    for p in range(PARTS):
        begin(up_copies(p))

    slot = lax.broadcasted_iota(jnp.int32, (slots, 2 * rows), 0)
    lane = lax.broadcasted_iota(jnp.int32, (slots, 2 * rows), 1)
    slot_expert, slot_step, slot_cap = slot // rows, slot % (rows // 2) // CAP, slot % CAP
    lane_step = lane % rows // per_step
    named = jnp.zeros((slots, 2 * rows), jnp.float32)
    gate = jnp.zeros((slots, 2 * rows), jnp.float32)
    for k in range(TOPK):
        ids = jnp.concatenate([ids_ref[k, s : s + 1, :] for s in range(steps)] * 2, axis=1)
        gates = gates_ref[k].astype(jnp.float32)
        gates = jnp.concatenate([gates[s : s + 1, :] for s in range(steps)] * 2, axis=1)
        match = ids == slot_expert
        named = named + jnp.where(match, 1.0, 0.0)
        gate = gate + jnp.where(match, gates, 0.0)
    before = lax.broadcasted_iota(jnp.int32, (2 * rows, 2 * rows), 0)
    after = lax.broadcasted_iota(jnp.int32, (2 * rows, 2 * rows), 1)
    earlier = jnp.where((before // per_step == after // per_step) & (before < after), 1.0, 0.0)
    rank = jnp.dot(
        named.astype(jnp.bfloat16), earlier.astype(jnp.bfloat16), preferred_element_type=jnp.float32
    )
    here = (rank == slot_cap.astype(jnp.float32)) & (lane_step == slot_step)
    placed = jnp.where(here, named, 0.0)
    gate = jnp.where(here, gate, 0.0)
    low = slot % rows < rows // 2
    weight = jnp.where((lane < rows) == low, gate, 0.0)
    eye_r = lax.broadcasted_iota(jnp.int32, (slots, slots), 0)
    eye_c = lax.broadcasted_iota(jnp.int32, (slots, slots), 1)
    eye = jnp.where(eye_r == eye_c, 1.0, 0.0).astype(jnp.bfloat16)
    mix[...] = lax.dot_general(
        weight.astype(jnp.bfloat16), eye, (((0,), (0,)), ((), ())), preferred_element_type=jnp.float32
    ).astype(jnp.bfloat16)
    own_r = lax.broadcasted_iota(jnp.int32, (rows, rows), 0)
    own_c = lax.broadcasted_iota(jnp.int32, (rows, rows), 1)
    pick[0:slots] = placed[:, :rows]
    pick[slots : slots + rows] = jnp.where(own_r == own_c, 1.0, 0.0)

    def halved(width):
        return lax.broadcasted_iota(jnp.int32, (slots, width), 0) % rows < rows // 2

    def lay_out(p):
        at, part = parts[p]
        half = part // 2
        chooser = pick[...].astype(jnp.bfloat16)
        x = jnp.concatenate(
            [tok_ref[s, :, at : at + part].astype(jnp.float32) for s in range(steps)], axis=0
        ).astype(jnp.bfloat16)
        a = jnp.dot(chooser, x[:, :half], preferred_element_type=jnp.float32)
        b = jnp.dot(chooser, x[:, half:], preferred_element_type=jnp.float32)
        block = jnp.where(halved(half), a[:slots], b[:slots]).reshape(chips, rows, half)
        dsp[p, :, :, 0:half] = block.astype(jnp.bfloat16)
        xs[p, core, xx, :, 0:half] = a[slots:].astype(jnp.bfloat16)
        xs[p, core, xx, :, half:part] = b[slots:].astype(jnp.bfloat16)
        xr[p, core, me, :, 0:half] = dsp[p, me, :, 0:half]

    def half_of(p):
        return pl.ds(0, parts[p][1] // 2)

    def part_of(p):
        return pl.ds(0, parts[p][1])

    def slot_send(p, i):
        return remote(
            dsp.at[p, chip_of(i), :, half_of(p)], xr.at[p, core, me, :, half_of(p)], d_send.at[p, i], d_recv.at[p, me], peer_of(i)
        )

    def share_send(p):
        return remote(
            xs.at[p, core, xx, :, part_of(p)], xs.at[p, core, xx, :, part_of(p)],
            sx_send.at[p], sx_recv.at[p], x_peer,
        )

    def slot_pass(p):
        block = xr.at[p, core, :, :, half_of(p)]
        return remote(block, block, f_send.at[p], f_recv.at[p], core_peer)

    def share_pass(p):
        block = xs.at[p, core, :, :, part_of(p)]
        return remote(block, block, sc_send.at[p], sc_recv.at[p], core_peer)

    for p in range(PARTS):
        lay_out(p)
    pl.semaphore_wait(barrier, len(away) + 1)
    for p in range(PARTS):
        for i in range(len(away)):
            slot_send(p, i).start()
        share_send(p).start()

    def landed(ref, sem):
        pltpu.make_async_copy(ref, ref, sem).wait()

    def forward(p):
        landed(xs.at[p, core, 1 - xx, :, part_of(p)], sx_recv.at[p])
        share_pass(p).start()
        for i in range(len(away)):
            landed(xr.at[p, core, chip_of(i), :, half_of(p)], d_recv.at[p, chip_of(i)])
        slot_pass(p).start()

    def settle(p):
        landed(xs.at[p, 1 - core, :, :, part_of(p)], sc_recv.at[p])
        landed(xr.at[p, 1 - core, :, :, half_of(p)], f_recv.at[p])

    row_id = lax.broadcasted_iota(jnp.int32, (LANES, 2 * WIDE), 0)
    col_id = lax.broadcasted_iota(jnp.int32, (LANES, 2 * WIDE), 1)
    hit = (col_id == 2 * row_id) | (col_id == WIDE + 2 * row_id + 1)
    spread = jnp.where(hit, 1.0, 0.0).astype(jnp.bfloat16)
    first = lax.broadcasted_iota(jnp.int32, (slots, LANES), 0) % rows < rows // 2
    shared_rows = 4 * rows

    def expand(p):
        start, part = parts[p]
        half = part // 2
        for j in range(half // LANES):
            cols = slice(j * LANES, (j + 1) * LANES)
            b0 = xr[p, 0, :, :, cols].astype(jnp.float32).reshape(slots, LANES)
            b1 = xr[p, 1, :, :, cols].astype(jnp.float32).reshape(slots, LANES)
            pieces = [
                jnp.where(first, b0, pltpu.roll(b1, rows // 2, 0)),
                jnp.where(first, pltpu.roll(b0, slots - rows // 2, 0), b1),
            ]
            for h in range(2):
                at = h * half + j * LANES
                piece = xs[p, :, :, :, at : at + LANES].astype(jnp.float32)
                pieces.append(piece.reshape(shared_rows, LANES))
            mixed = jnp.concatenate(pieces, axis=0).astype(jnp.bfloat16)
            both = jnp.dot(mixed, spread, preferred_element_type=jnp.float32).astype(jnp.bfloat16)
            for h in range(2):
                to = 2 * (start + h * half + j * LANES)
                for g in range(2):
                    ways = slice(g * WIDE, (g + 1) * WIDE)
                    x2[g * slots : (g + 1) * slots, to : to + WIDE] = both[
                        h * slots : (h + 1) * slots, ways
                    ]
                    x2s[g * shared_rows : (g + 1) * shared_rows, to : to + WIDE] = both[
                        2 * slots + h * shared_rows : 2 * slots + (h + 1) * shared_rows, ways
                    ]

    def multiply(p):
        for copy in up_copies(p):
            copy.wait()
        span = pl.ds(2 * parts[p][0], 2 * parts[p][1])
        w = jnp.concatenate([wb[t, span] for t in range(tiles)], axis=1)
        d = jnp.dot(x2[:, span], w, preferred_element_type=jnp.float32)
        if p + 1 < PARTS:
            forward(p + 1)
        w = jnp.concatenate([wsb[t, span] for t in range(share_tiles)], axis=1)
        ds = jnp.dot(x2s[:, span], w, preferred_element_type=jnp.float32)
        if p == 0:
            acc[...] = d
            accs[...] = ds
        else:
            acc[...] += d
            accs[...] += ds

    def freed_by(q):
        end = (downs[q][0] + downs[q][1]) // LANES
        last = max(-(-end // tiles) * units, -(-end // share_tiles) * share)
        return next(p for p in range(PARTS) if 2 * sum(parts[p]) >= last)

    forward(0)
    for p in range(PARTS):
        settle(p)
        expand(p)
        multiply(p)
        for q in range(DOWNS):
            if freed_by(q) == p:
                begin(down_copies(q))

    def hidden(both, m):
        return (jax.nn.silu(both[:m]) * both[m:]).astype(jnp.bfloat16)

    hid[...] = hidden(acc[...], slots)
    hids[...] = hidden(accs[...], shared_rows)

    def wide_of(q):
        return pl.ds(0, downs[q][1] // 2)

    def core_copy(q):
        cols = wide_of(q)
        return remote(
            s1.at[q, :, cols], r1.at[q, :, cols], c_send.at[q], c_recv.at[q], core_peer
        )

    def slot_copy(q, i):
        return remote(
            s2.at[q, chip_of(i), :, wide_of(q)], r2.at[q, me, :, wide_of(q)],
            z_send.at[q, i], z_recv.at[q, me], peer_of(i),
        )

    def x_copy(q):
        return remote(
            s2.at[q, pl.ds(chips + 2 * (1 - xx), 2), :, wide_of(q)],
            r2.at[q, pl.ds(chips, 2), :, wide_of(q)],
            x_send.at[q],
            x_recv.at[q],
            x_peer,
        )

    mine = 2 * rows

    def stage_one(q):
        for copy in down_copies(q):
            copy.wait()
        cs, wide = down_range(q), downs[q][1] // 2
        top = halved(wide)
        w = jnp.concatenate([down_place(c)[...] for c in cs], axis=1)
        a = jnp.dot(hid[...], w, preferred_element_type=jnp.float32)
        w = jnp.concatenate([share_place(c)[...] for c in cs], axis=1)
        b = jnp.dot(hids[...], w, preferred_element_type=jnp.float32)
        lo, hi = a[:, :wide], a[:, wide:]
        t0 = jnp.where(top, lo, pltpu.roll(hi, rows // 2, 0))
        t1 = jnp.where(top, pltpu.roll(lo, slots - rows // 2, 0), hi)

        def pack(t, u):
            return jnp.concatenate(
                [t, u[:rows, :wide], u[:rows, wide:], u[rows:, :wide], u[rows:, wide:]], axis=0
            )

        p0, p1 = pack(t0, b[:mine]), pack(t1, b[mine:])
        s1[q, :, 0:wide] = jnp.where(core == 0, p1, p0).astype(jnp.bfloat16)
        core_copy(q).start()
        k1[q, :, 0:wide] = jnp.where(core == 0, p0, p1)

    def stage_two(q):
        core_copy(q).wait_recv()
        wide = downs[q][1] // 2
        p = k1[q, :, 0:wide] + r1[q, :, 0:wide].astype(jnp.float32)
        s2[q, :, :, 0:wide] = p.reshape(chips + 4, rows, wide).astype(jnp.bfloat16)
        for i in range(len(away)):
            slot_copy(q, i).start()
        x_copy(q).start()
        r2[q, me, :, 0:wide] = s2[q, me, :, 0:wide]

    def stage_three(q):
        at, wide = downs[q][0], downs[q][1] // 2
        for i in range(len(away)):
            landed(r2.at[q, chip_of(i), :, wide_of(q)], z_recv.at[q, chip_of(i)])
        x_copy(q).wait_recv()
        back = r2[q, 0:chips, :, 0:wide].astype(jnp.float32).reshape(slots, wide).astype(jnp.bfloat16)
        both = jnp.dot(mix[...], back, preferred_element_type=jnp.float32)
        for h in range(2):
            p = both[h * rows : (h + 1) * rows]
            p = p + r2[q, chips + h, :, 0:wide].astype(jnp.float32)
            p = p + s2[q, chips + 2 * xx + h, :, 0:wide].astype(jnp.float32)
            p = p.astype(jnp.bfloat16).astype(jnp.float32)
            to = at + h * wide
            for s in range(steps):
                out_ref[s, :, to : to + wide] = p[s * per_step : (s + 1) * per_step].astype(
                    jnp.bfloat16
                )

    for step in range(DOWNS + 2):
        if step >= 2:
            stage_two(step - 2)
        if step < DOWNS:
            stage_one(step)
    for q in range(DOWNS):
        stage_three(q)

    for p in range(PARTS):
        for i in range(len(away)):
            slot_send(p, i).wait_send()
        for copy in (share_send(p), slot_pass(p), share_pass(p)):
            copy.wait_send()
    for q in range(DOWNS):
        core_copy(q).wait_send()
        x_copy(q).wait_send()
        for i in range(len(away)):
            slot_copy(q, i).wait_send()


def scratch_of(n, rows, depth, units):
    chips = n // 2
    slots, shared = chips * rows, 4 * rows
    tiles, share_tiles = units // LANES, units // (2 * LANES)
    part = max(size for _, size in spans(depth, PART_UNITS))
    down = max(size for _, size in spans(depth, DOWN_UNITS))
    half, wide, down_tiles = part // 2, down // 2, down // LANES
    bf, fl = jnp.bfloat16, jnp.float32
    packed = slots + 4 * rows
    buffers = [
        ((tiles, 2 * depth, LANES), bf),
        ((share_tiles, 2 * depth, LANES), bf),
        ((2 * slots, 2 * depth), bf),
        ((2 * shared, 2 * depth), bf),
        ((2 * slots, units), fl),
        ((2 * shared, share_tiles * LANES), fl),
        ((slots, units), bf),
        ((shared, share_tiles * LANES), bf),
        ((slots + rows, rows), fl),
        ((2 * rows, slots), bf),
        ((PARTS, chips, rows, half), bf),
        ((PARTS, 2, chips, rows, half), bf),
        ((PARTS, 2, 2, rows, part), bf),
        ((DOWNS, packed, wide), fl),
        ((DOWNS, packed, wide), bf),
        ((DOWNS, packed, wide), bf),
        ((DOWNS, chips + 4, rows, wide), bf),
        ((DOWNS, chips + 2, rows, wide), bf),
    ]
    dma = pltpu.SemaphoreType.DMA
    sems = [
        dma((PARTS, tiles + share_tiles)), dma((DOWNS, 2 * down_tiles)),
        dma((PARTS, chips)), dma((PARTS, chips)),
        dma((PARTS,)), dma((PARTS,)), dma((PARTS,)), dma((PARTS,)), dma((PARTS,)), dma((PARTS,)),
        dma((DOWNS,)), dma((DOWNS,)), dma((DOWNS, chips)), dma((DOWNS, chips)),
        dma((DOWNS,)), dma((DOWNS,)),
    ]
    return [pltpu.VMEM(shape, kind) for shape, kind in buffers] + sems


def local_fused(tokens, expert_ids, gate_weights, w_gate_up, w_down, shared_gate_up, shared_down):
    n = lax.axis_size("fast")
    steps, per_step, depth = tokens.shape
    rows, units = steps * per_step, w_gate_up.shape[2]
    whole = pl.BlockSpec(memory_space=pltpu.VMEM)
    there = pl.BlockSpec(memory_space=pl.ANY)
    return pl.pallas_call(
        functools.partial(fused_kernel, n),
        out_shape=jax.ShapeDtypeStruct((steps, per_step, depth), jnp.bfloat16),
        in_specs=[whole, whole, whole, there, there, there, there],
        out_specs=whole,
        scratch_shapes=scratch_of(n, rows, depth, units),
        compiler_params=pltpu.CompilerParams(
            collective_id=0, has_side_effects=True, vmem_limit_bytes=67043328
        ),
    )(
        tokens,
        jnp.transpose(expert_ids, (2, 0, 1)),
        jnp.transpose(gate_weights, (2, 0, 1)),
        w_gate_up, w_down, shared_gate_up, shared_down,
    )


def local(tokens, expert_ids, gate_weights, w_gate_up, w_down, shared_gate_up, shared_down):
    n = lax.axis_size("fast")
    steps, per_step, depth = tokens.shape
    units = w_gate_up.shape[2]
    fits = n == 2 * EXPERTS and steps == STEPS and per_step == 2 * CAP
    fits = fits and units == EXPERTS * LANES and depth == 2 * LANES * sum(PART_UNITS) == 2 * LANES * sum(DOWN_UNITS)
    run = local_fused if fits else local_exchange
    return run(
        tokens, expert_ids, gate_weights, w_gate_up, w_down, shared_gate_up, shared_down
    )


def solution(mesh):
    placed = (
        P(None, ("rep", "fast"), None),
        P(None, ("rep", "fast"), None),
        P(None, ("rep", "fast"), None),
        P(None, None, "fast"),
        P("fast", None),
        P(None, None, "fast"),
        P("fast", None),
    )
    return jax.shard_map(
        local, mesh=mesh, in_specs=placed, out_specs=P(None, ("rep", "fast"), None), check_vma=False
    )
```

```python
import functools
import math

import jax
import jax.numpy as jnp
from jax import lax
from jax.experimental import pallas as pl
from jax.experimental.pallas import tpu as pltpu
from jax.sharding import PartitionSpec as P

EXPERTS = 8
TOPK = 3
STEPS = 2
CAP = 2
LANES = 128
WIDE = 256
PART_UNITS = (7, 7, 7, 7)
DOWN_UNITS = (7, 7, 7, 7)
PARTS = len(PART_UNITS)
DOWNS = len(DOWN_UNITS)


def slot_tables(step_tokens, step_ids, step_gates):
    tok_count = step_ids.shape[0]
    flat_ids = step_ids.reshape(tok_count * TOPK)
    expert_hit = (flat_ids[:, None] == jnp.arange(EXPERTS, dtype=jnp.int32)[None, :]).astype(
        jnp.int32
    )
    slot_rank = jnp.sum((jnp.cumsum(expert_hit, axis=0) - expert_hit) * expert_hit, axis=1)
    slot_index = flat_ids * CAP + slot_rank
    placed = (slot_index[:, None] == jnp.arange(EXPERTS * CAP, dtype=jnp.int32)[None, :]).astype(
        jnp.float32
    )
    selector = jnp.sum(placed.reshape(tok_count, TOPK, EXPERTS * CAP), axis=1)
    blocks = jnp.einsum(
        "ts,td->sd", selector.astype(jnp.bfloat16), step_tokens, preferred_element_type=jnp.float32
    ).astype(jnp.bfloat16)
    share_row = jnp.broadcast_to(
        (jnp.arange(TOPK) == 0).astype(jnp.float32)[None, :], (tok_count, TOPK)
    ).reshape(-1)
    gate_row = step_gates.astype(jnp.float32).reshape(-1)
    slot_coefs = jnp.einsum(
        "rs,rc->sc",
        placed,
        jnp.stack([gate_row, share_row], axis=1),
        precision=lax.Precision.HIGHEST,
    ).astype(jnp.bfloat16)
    return (blocks.reshape(EXPERTS, CAP, -1), slot_coefs.reshape(EXPERTS, CAP, 2), selector)


def send_out(blocks, slot_coefs, group_size):
    spread = jnp.repeat(blocks, group_size, axis=0)
    spread_coefs = jnp.repeat(slot_coefs, group_size, axis=0)
    arrived, arrived_coefs = (
        lax.all_to_all(spread, "fast", split_axis=0, concat_axis=0, tiled=True),
        lax.all_to_all(spread_coefs, "fast", split_axis=0, concat_axis=0, tiled=True),
    )
    return (arrived, arrived_coefs)


def expert_work(arrived, arrived_coefs, weights):
    w_gate_up, w_down, shared_gate_up, shared_down = weights
    model_width = arrived.shape[-1]
    hidden_size = w_down.shape[0]
    flat_rows = arrived.reshape(-1, model_width)
    flat_coef = arrived_coefs.reshape(-1, 2).astype(jnp.float32)
    row_count = flat_rows.shape[0]
    block_rows = math.gcd(row_count, 512)
    routed_up = w_gate_up.reshape(model_width, 2 * hidden_size)
    common_up = shared_gate_up.reshape(model_width, 2 * hidden_size)

    def one_block(block_pair):
        row_block, slot_coef = block_pair
        routed = jnp.dot(row_block, routed_up, preferred_element_type=jnp.float32)
        routed_hidden = (jax.nn.silu(routed[:, :hidden_size]) * routed[:, hidden_size:]).astype(
            jnp.bfloat16
        )
        common = jnp.dot(row_block, common_up, preferred_element_type=jnp.float32)
        common_hidden = (jax.nn.silu(common[:, :hidden_size]) * common[:, hidden_size:]).astype(
            jnp.bfloat16
        )
        result = slot_coef[:, 0:1] * jnp.dot(
            routed_hidden, w_down, preferred_element_type=jnp.float32
        )
        result = result + slot_coef[:, 1:2] * jnp.dot(
            common_hidden, shared_down, preferred_element_type=jnp.float32
        )
        return result.astype(jnp.bfloat16)

    outcome = lax.map(
        one_block,
        (flat_rows.reshape(-1, block_rows, model_width), flat_coef.reshape(-1, block_rows, 2)),
    )
    return outcome.reshape(arrived.shape)


def round_trip(blocks, slot_coefs, weights, group_size):
    arrived, arrived_coefs = send_out(blocks, slot_coefs, group_size)
    partials = expert_work(arrived, arrived_coefs, weights)
    returned = lax.all_to_all(partials, "fast", split_axis=0, concat_axis=0, tiled=True)
    slot_count = blocks.shape[1]
    return returned.reshape(EXPERTS, group_size, slot_count, -1).astype(jnp.float32).sum(axis=1)


def finish(selector, summed):
    flat_sums = summed.reshape(selector.shape[1], -1)
    return jnp.dot(
        selector, flat_sums, precision=lax.Precision.HIGHEST, preferred_element_type=jnp.float32
    ).astype(jnp.bfloat16)


def local_exchange(tokens, expert_ids, gate_weights, w_gate_up, w_down, shared_gate_up, shared_down):
    group_size = lax.axis_size("fast") // EXPERTS
    weights = (w_gate_up, w_down, shared_gate_up, shared_down)
    prepared = [
        slot_tables(tokens[step_index], expert_ids[step_index], gate_weights[step_index])
        for step_index in range(STEPS)
    ]
    outputs = []
    model_width = tokens.shape[-1]
    blocks = jnp.stack([member[0] for member in prepared], axis=1).reshape(
        EXPERTS, STEPS * CAP, model_width
    )
    slot_coefs = jnp.stack([member[1] for member in prepared], axis=1).reshape(
        EXPERTS, STEPS * CAP, 2
    )
    summed = round_trip(blocks, slot_coefs, weights, group_size).reshape(
        EXPERTS, STEPS, CAP, model_width
    )
    for step_index in range(STEPS):
        outputs.append(finish(prepared[step_index][2], summed[:, step_index]))
    return jnp.stack(outputs, axis=0)


def spans(size, units):
    unit = size // sum(units)
    return [(unit * sum(units[:i]), unit * count) for i, count in enumerate(units)]


def fused_kernel(
    n,
    tok_ref, ids_ref, gates_ref, wg_ref, wd_ref, sg_ref, sd_ref, out_ref,
    wb, wsb, x2, x2s, acc, accs, hid, hids, pick, mix,
    dsp, xr, xs, k1, s1, r1, s2, r2,
    up_sem, down_sem, d_send, d_recv, f_send, f_recv, sx_send, sx_recv, sc_send, sc_recv,
    c_send, c_recv, z_send, z_recv, x_send, x_recv, n_send, sn_send, sn_recv, y_send, y_recv,
):
    depth, _, units = wg_ref.shape
    steps, per_step, _ = tok_ref.shape
    rows = steps * per_step
    zs, chips = n // 4, n // 2
    slots = chips * rows
    tiles, share_tiles = units // LANES, units // (2 * LANES)
    share = share_tiles * LANES
    parts, downs = spans(depth, PART_UNITS), spans(depth, DOWN_UNITS)
    f = lax.axis_index("fast")
    core, xx, zz = f % 2, (f // 2) % 2, f // 4
    me = f // 2
    core_peer = {"fast": f + 1 - 2 * core}
    x_peer = {"fast": f + 2 - 4 * xx + 1 - 2 * core}
    away = [(dz, dx) for dz in range(1, zs) for dx in (0, 1)] + [(0, 1)]

    def chip_of(i):
        dz, dx = away[i]
        return ((zz + dz) % zs) * 2 + (xx + dx) % 2

    def peer_of(i):
        return {"fast": chip_of(i) * 2 + 1 - core}

    def remote(src, dst, ssem, rsem, peer):
        return pltpu.make_async_remote_copy(
            src_ref=src, dst_ref=dst, send_sem=ssem, recv_sem=rsem,
            device_id=peer, device_id_type=pl.DeviceIdType.MESH,
        )

    barrier = pltpu.get_barrier_semaphore()
    for peer in [core_peer] + [peer_of(i) for i in range(len(away))]:
        pl.semaphore_signal(barrier, inc=1, device_id=peer, device_id_type=pl.DeviceIdType.MESH)

    flat_g = wg_ref.reshape(2 * depth, units)
    flat_s = sg_ref.reshape(2 * depth, units)
    share_at = pl.multiple_of(xx * share, share)

    def up_copies(p):
        span = pl.ds(2 * parts[p][0], 2 * parts[p][1])
        for t in range(tiles):
            yield pltpu.make_async_copy(
                flat_g.at[span, pl.ds(t * LANES, LANES)], wb.at[t, span], up_sem.at[p, t]
            )
        for t in range(share_tiles):
            yield pltpu.make_async_copy(
                flat_s.at[span, pl.ds(share_at + t * LANES, LANES)],
                wsb.at[t, span],
                up_sem.at[p, tiles + t],
            )

    def down_place(c):
        return wb.at[c % tiles, pl.ds((c // tiles) * units, units)]

    def share_place(c):
        return wsb.at[c % share_tiles, pl.ds((c // share_tiles) * share, share)]

    def down_range(q):
        at, size = downs[q]
        return range(at // LANES, (at + size) // LANES)

    def down_copies(q):
        for i, c in enumerate(down_range(q)):
            cols = pl.ds(c * LANES, LANES)
            yield pltpu.make_async_copy(wd_ref.at[:, cols], down_place(c), down_sem.at[q, i])
            yield pltpu.make_async_copy(
                sd_ref.at[pl.ds(share_at, share), cols],
                share_place(c),
                down_sem.at[q, len(down_range(q)) + i],
            )

    def begin(copies):
        for copy in copies:
            copy.start()

    for p in range(PARTS):
        begin(up_copies(p))

    slot = lax.broadcasted_iota(jnp.int32, (slots, 2 * rows), 0)
    lane = lax.broadcasted_iota(jnp.int32, (slots, 2 * rows), 1)
    slot_expert, slot_step, slot_cap = slot // rows, slot % (rows // 2) // CAP, slot % CAP
    lane_step = lane % rows // per_step
    named = jnp.zeros((slots, 2 * rows), jnp.float32)
    gate = jnp.zeros((slots, 2 * rows), jnp.float32)
    for k in range(TOPK):
        ids = jnp.concatenate([ids_ref[k, s : s + 1, :] for s in range(steps)] * 2, axis=1)
        gates = gates_ref[k].astype(jnp.float32)
        gates = jnp.concatenate([gates[s : s + 1, :] for s in range(steps)] * 2, axis=1)
        match = ids == slot_expert
        named = named + jnp.where(match, 1.0, 0.0)
        gate = gate + jnp.where(match, gates, 0.0)
    before = lax.broadcasted_iota(jnp.int32, (2 * rows, 2 * rows), 0)
    after = lax.broadcasted_iota(jnp.int32, (2 * rows, 2 * rows), 1)
    earlier = jnp.where((before // per_step == after // per_step) & (before < after), 1.0, 0.0)
    rank = jnp.dot(
        named.astype(jnp.bfloat16), earlier.astype(jnp.bfloat16), preferred_element_type=jnp.float32
    )
    here = (rank == slot_cap.astype(jnp.float32)) & (lane_step == slot_step)
    placed = jnp.where(here, named, 0.0)
    gate = jnp.where(here, gate, 0.0)
    low = slot % rows < rows // 2
    weight = jnp.where((lane < rows) == low, gate, 0.0)
    eye_r = lax.broadcasted_iota(jnp.int32, (slots, slots), 0)
    eye_c = lax.broadcasted_iota(jnp.int32, (slots, slots), 1)
    eye = jnp.where(eye_r == eye_c, 1.0, 0.0).astype(jnp.bfloat16)
    mix[...] = lax.dot_general(
        weight.astype(jnp.bfloat16), eye, (((0,), (0,)), ((), ())), preferred_element_type=jnp.float32
    ).astype(jnp.bfloat16)
    own_r = lax.broadcasted_iota(jnp.int32, (rows, rows), 0)
    own_c = lax.broadcasted_iota(jnp.int32, (rows, rows), 1)
    pick[0:slots] = placed[:, :rows]
    pick[slots : slots + rows] = jnp.where(own_r == own_c, 1.0, 0.0)

    def halved(width):
        return lax.broadcasted_iota(jnp.int32, (slots, width), 0) % rows < rows // 2

    def lay_out(p):
        at, part = parts[p]
        half = part // 2
        chooser = pick[...].astype(jnp.bfloat16)
        x = jnp.concatenate(
            [tok_ref[s, :, at : at + part].astype(jnp.float32) for s in range(steps)], axis=0
        ).astype(jnp.bfloat16)
        a = jnp.dot(chooser, x[:, :half], preferred_element_type=jnp.float32)
        b = jnp.dot(chooser, x[:, half:], preferred_element_type=jnp.float32)
        block = jnp.where(halved(half), a[:slots], b[:slots]).reshape(chips, rows, half)
        dsp[p, :, :, 0:half] = block.astype(jnp.bfloat16)
        xs[p, core, xx, :, 0:half] = a[slots:].astype(jnp.bfloat16)
        xs[p, core, xx, :, half:part] = b[slots:].astype(jnp.bfloat16)

    def half_of(p):
        return pl.ds(0, parts[p][1] // 2)

    def part_of(p):
        return pl.ds(0, parts[p][1])

    def slot_send(p, i):
        return remote(
            dsp.at[p, chip_of(i), :, half_of(p)], xr.at[p, core, me, :, half_of(p)], d_send.at[p, i], d_recv.at[p, me], peer_of(i)
        )

    def share_send(p):
        return remote(
            xs.at[p, core, xx, :, part_of(p)], xs.at[p, core, xx, :, part_of(p)],
            sx_send.at[p], sx_recv.at[p], x_peer,
        )

    def slot_near(p):
        return remote(
            dsp.at[p, me, :, half_of(p)], xr.at[p, core, me, :, half_of(p)],
            n_send.at[p], d_recv.at[p, me], core_peer,
        )

    def share_near(p):
        block = xs.at[p, core, xx, :, part_of(p)]
        return remote(block, block, sn_send.at[p], sn_recv.at[p], core_peer)

    def slot_pass(p):
        block = xr.at[p, 1 - core, :, :, half_of(p)]
        return remote(block, block, f_send.at[p], f_recv.at[p], core_peer)

    def share_pass(p):
        block = xs.at[p, 1 - core, 1 - xx, :, part_of(p)]
        return remote(block, block, sc_send.at[p], sc_recv.at[p], core_peer)

    for p in range(PARTS):
        lay_out(p)
    pl.semaphore_wait(barrier, len(away) + 1)
    for p in range(PARTS):
        for i in range(len(away)):
            slot_send(p, i).start()
        share_send(p).start()
        slot_near(p).start()
        share_near(p).start()

    def landed(ref, sem):
        pltpu.make_async_copy(ref, ref, sem).wait()

    def forward(p):
        landed(xs.at[p, 1 - core, 1 - xx, :, part_of(p)], sx_recv.at[p])
        share_pass(p).start()
        for i in range(len(away)):
            landed(xr.at[p, 1 - core, chip_of(i), :, half_of(p)], d_recv.at[p, chip_of(i)])
        landed(xr.at[p, 1 - core, me, :, half_of(p)], d_recv.at[p, me])
        slot_pass(p).start()

    def settle(p):
        landed(xs.at[p, 1 - core, xx, :, part_of(p)], sn_recv.at[p])
        landed(xs.at[p, core, 1 - xx, :, part_of(p)], sc_recv.at[p])
        landed(xr.at[p, core, :, :, half_of(p)], f_recv.at[p])

    row_id = lax.broadcasted_iota(jnp.int32, (LANES, 2 * WIDE), 0)
    col_id = lax.broadcasted_iota(jnp.int32, (LANES, 2 * WIDE), 1)
    hit = (col_id == 2 * row_id) | (col_id == WIDE + 2 * row_id + 1)
    spread = jnp.where(hit, 1.0, 0.0).astype(jnp.bfloat16)
    first = lax.broadcasted_iota(jnp.int32, (slots, LANES), 0) % rows < rows // 2
    shared_rows = 4 * rows

    def expand(p):
        start, part = parts[p]
        half = part // 2
        for j in range(half // LANES):
            cols = slice(j * LANES, (j + 1) * LANES)
            b0 = xr[p, 0, :, :, cols].astype(jnp.float32).reshape(slots, LANES)
            b1 = xr[p, 1, :, :, cols].astype(jnp.float32).reshape(slots, LANES)
            pieces = [
                jnp.where(first, b0, pltpu.roll(b1, rows // 2, 0)),
                jnp.where(first, pltpu.roll(b0, slots - rows // 2, 0), b1),
            ]
            for h in range(2):
                at = h * half + j * LANES
                piece = xs[p, :, :, :, at : at + LANES].astype(jnp.float32)
                pieces.append(piece.reshape(shared_rows, LANES))
            mixed = jnp.concatenate(pieces, axis=0).astype(jnp.bfloat16)
            both = jnp.dot(mixed, spread, preferred_element_type=jnp.float32).astype(jnp.bfloat16)
            for h in range(2):
                to = 2 * (start + h * half + j * LANES)
                for g in range(2):
                    ways = slice(g * WIDE, (g + 1) * WIDE)
                    x2[g * slots : (g + 1) * slots, to : to + WIDE] = both[
                        h * slots : (h + 1) * slots, ways
                    ]
                    x2s[g * shared_rows : (g + 1) * shared_rows, to : to + WIDE] = both[
                        2 * slots + h * shared_rows : 2 * slots + (h + 1) * shared_rows, ways
                    ]

    def multiply(p):
        for copy in up_copies(p):
            copy.wait()
        span = pl.ds(2 * parts[p][0], 2 * parts[p][1])
        w = jnp.concatenate([wb[t, span] for t in range(tiles)], axis=1)
        d = jnp.dot(x2[:, span], w, preferred_element_type=jnp.float32)
        if p + 1 < PARTS:
            forward(p + 1)
        w = jnp.concatenate([wsb[t, span] for t in range(share_tiles)], axis=1)
        ds = jnp.dot(x2s[:, span], w, preferred_element_type=jnp.float32)
        if p == 0:
            acc[...] = d
            accs[...] = ds
        else:
            acc[...] += d
            accs[...] += ds

    def freed_by(q):
        end = (downs[q][0] + downs[q][1]) // LANES
        last = max(-(-end // tiles) * units, -(-end // share_tiles) * share)
        return next(p for p in range(PARTS) if 2 * sum(parts[p]) >= last)

    forward(0)
    for p in range(PARTS):
        settle(p)
        expand(p)
        multiply(p)
        for q in range(DOWNS):
            if freed_by(q) == p:
                begin(down_copies(q))

    def hidden(both, m):
        return (jax.nn.silu(both[:m]) * both[m:]).astype(jnp.bfloat16)

    hid[...] = hidden(acc[...], slots)
    hids[...] = hidden(accs[...], shared_rows)

    def wide_of(q):
        return pl.ds(0, downs[q][1] // 2)

    def core_copy(q):
        cols = wide_of(q)
        return remote(
            s1.at[q, :, cols], r1.at[q, :, cols], c_send.at[q], c_recv.at[q], core_peer
        )

    def slot_copy(q, i):
        return remote(
            s2.at[q, chip_of(i), :, wide_of(q)], r2.at[q, me, :, wide_of(q)],
            z_send.at[q, i], z_recv.at[q, me], peer_of(i),
        )

    def slot_home(q):
        return remote(
            s2.at[q, me, :, wide_of(q)], r2.at[q, me, :, wide_of(q)],
            z_send.at[q, len(away)], z_recv.at[q, me], core_peer,
        )

    def share_home(q):
        return remote(
            s2.at[q, pl.ds(chips + 2 * xx, 2), :, wide_of(q)],
            r2.at[q, pl.ds(chips + 2, 2), :, wide_of(q)],
            y_send.at[q], y_recv.at[q], core_peer,
        )

    def x_copy(q):
        return remote(
            s2.at[q, pl.ds(chips + 2 * (1 - xx), 2), :, wide_of(q)],
            r2.at[q, pl.ds(chips, 2), :, wide_of(q)],
            x_send.at[q],
            x_recv.at[q],
            x_peer,
        )

    mine = 2 * rows

    def stage_one(q):
        for copy in down_copies(q):
            copy.wait()
        cs, wide = down_range(q), downs[q][1] // 2
        top = halved(wide)
        w = jnp.concatenate([down_place(c)[...] for c in cs], axis=1)
        a = jnp.dot(hid[...], w, preferred_element_type=jnp.float32)
        w = jnp.concatenate([share_place(c)[...] for c in cs], axis=1)
        b = jnp.dot(hids[...], w, preferred_element_type=jnp.float32)
        lo, hi = a[:, :wide], a[:, wide:]
        t0 = jnp.where(top, lo, pltpu.roll(hi, rows // 2, 0))
        t1 = jnp.where(top, pltpu.roll(lo, slots - rows // 2, 0), hi)

        def pack(t, u):
            return jnp.concatenate(
                [t, u[:rows, :wide], u[:rows, wide:], u[rows:, :wide], u[rows:, wide:]], axis=0
            )

        p0, p1 = pack(t0, b[:mine]), pack(t1, b[mine:])
        s1[q, :, 0:wide] = jnp.where(core == 0, p0, p1).astype(jnp.bfloat16)
        core_copy(q).start()
        k1[q, :, 0:wide] = jnp.where(core == 0, p1, p0)

    def stage_two(q):
        core_copy(q).wait_recv()
        wide = downs[q][1] // 2
        p = k1[q, :, 0:wide] + r1[q, :, 0:wide].astype(jnp.float32)
        s2[q, :, :, 0:wide] = p.reshape(chips + 4, rows, wide).astype(jnp.bfloat16)
        for i in range(len(away)):
            slot_copy(q, i).start()
        x_copy(q).start()
        slot_home(q).start()
        share_home(q).start()

    def stage_three(q):
        at, wide = downs[q][0], downs[q][1] // 2
        for i in range(len(away)):
            landed(r2.at[q, chip_of(i), :, wide_of(q)], z_recv.at[q, chip_of(i)])
        landed(r2.at[q, me, :, wide_of(q)], z_recv.at[q, me])
        x_copy(q).wait_recv()
        share_home(q).wait_recv()
        back = r2[q, 0:chips, :, 0:wide].astype(jnp.float32).reshape(slots, wide).astype(jnp.bfloat16)
        both = jnp.dot(mix[...], back, preferred_element_type=jnp.float32)
        for h in range(2):
            p = both[h * rows : (h + 1) * rows]
            p = p + r2[q, chips + h, :, 0:wide].astype(jnp.float32)
            p = p + r2[q, chips + 2 + h, :, 0:wide].astype(jnp.float32)
            p = p.astype(jnp.bfloat16).astype(jnp.float32)
            to = at + h * wide
            for s in range(steps):
                out_ref[s, :, to : to + wide] = p[s * per_step : (s + 1) * per_step].astype(
                    jnp.bfloat16
                )

    for step in range(DOWNS + 2):
        if step >= 2:
            stage_two(step - 2)
        if step < DOWNS:
            stage_one(step)
    for q in range(DOWNS):
        stage_three(q)

    for p in range(PARTS):
        for i in range(len(away)):
            slot_send(p, i).wait_send()
        for copy in (share_send(p), slot_pass(p), share_pass(p), slot_near(p), share_near(p)):
            copy.wait_send()
    for q in range(DOWNS):
        core_copy(q).wait_send()
        for copy in (x_copy(q), slot_home(q), share_home(q)):
            copy.wait_send()
        for i in range(len(away)):
            slot_copy(q, i).wait_send()


def scratch_of(n, rows, depth, units):
    chips = n // 2
    slots, shared = chips * rows, 4 * rows
    tiles, share_tiles = units // LANES, units // (2 * LANES)
    part = max(size for _, size in spans(depth, PART_UNITS))
    down = max(size for _, size in spans(depth, DOWN_UNITS))
    half, wide, down_tiles = part // 2, down // 2, down // LANES
    bf, fl = jnp.bfloat16, jnp.float32
    packed = slots + 4 * rows
    buffers = [
        ((tiles, 2 * depth, LANES), bf),
        ((share_tiles, 2 * depth, LANES), bf),
        ((2 * slots, 2 * depth), bf),
        ((2 * shared, 2 * depth), bf),
        ((2 * slots, units), fl),
        ((2 * shared, share_tiles * LANES), fl),
        ((slots, units), bf),
        ((shared, share_tiles * LANES), bf),
        ((slots + rows, rows), fl),
        ((2 * rows, slots), bf),
        ((PARTS, chips, rows, half), bf),
        ((PARTS, 2, chips, rows, half), bf),
        ((PARTS, 2, 2, rows, part), bf),
        ((DOWNS, packed, wide), fl),
        ((DOWNS, packed, wide), bf),
        ((DOWNS, packed, wide), bf),
        ((DOWNS, chips + 4, rows, wide), bf),
        ((DOWNS, chips + 4, rows, wide), bf),
    ]
    dma = pltpu.SemaphoreType.DMA
    sems = [
        dma((PARTS, tiles + share_tiles)), dma((DOWNS, 2 * down_tiles)),
        dma((PARTS, chips)), dma((PARTS, chips)),
        dma((PARTS,)), dma((PARTS,)), dma((PARTS,)), dma((PARTS,)), dma((PARTS,)), dma((PARTS,)),
        dma((DOWNS,)), dma((DOWNS,)), dma((DOWNS, chips)), dma((DOWNS, chips)),
        dma((DOWNS,)), dma((DOWNS,)), dma((PARTS,)), dma((PARTS,)), dma((PARTS,)),
        dma((DOWNS,)), dma((DOWNS,)),
    ]
    return [pltpu.VMEM(shape, kind) for shape, kind in buffers] + sems


def local_fused(tokens, expert_ids, gate_weights, w_gate_up, w_down, shared_gate_up, shared_down):
    n = lax.axis_size("fast")
    steps, per_step, depth = tokens.shape
    rows, units = steps * per_step, w_gate_up.shape[2]
    whole = pl.BlockSpec(memory_space=pltpu.VMEM)
    there = pl.BlockSpec(memory_space=pl.ANY)
    return pl.pallas_call(
        functools.partial(fused_kernel, n),
        out_shape=jax.ShapeDtypeStruct((steps, per_step, depth), jnp.bfloat16),
        in_specs=[whole, whole, whole, there, there, there, there],
        out_specs=whole,
        scratch_shapes=scratch_of(n, rows, depth, units),
        compiler_params=pltpu.CompilerParams(
            collective_id=0, has_side_effects=True, vmem_limit_bytes=67043328
        ),
    )(
        tokens,
        jnp.transpose(expert_ids, (2, 0, 1)),
        jnp.transpose(gate_weights, (2, 0, 1)),
        w_gate_up, w_down, shared_gate_up, shared_down,
    )


def local(tokens, expert_ids, gate_weights, w_gate_up, w_down, shared_gate_up, shared_down):
    n = lax.axis_size("fast")
    steps, per_step, depth = tokens.shape
    units = w_gate_up.shape[2]
    fits = n == 2 * EXPERTS and steps == STEPS and per_step == 2 * CAP
    fits = fits and units == EXPERTS * LANES and depth == 2 * LANES * sum(PART_UNITS) == 2 * LANES * sum(DOWN_UNITS)
    run = local_fused if fits else local_exchange
    return run(
        tokens, expert_ids, gate_weights, w_gate_up, w_down, shared_gate_up, shared_down
    )


def solution(mesh):
    placed = (
        P(None, ("rep", "fast"), None),
        P(None, ("rep", "fast"), None),
        P(None, ("rep", "fast"), None),
        P(None, None, "fast"),
        P("fast", None),
        P(None, None, "fast"),
        P("fast", None),
    )
    return jax.shard_map(
        local, mesh=mesh, in_specs=placed, out_specs=P(None, ("rep", "fast"), None), check_vma=False
    )
```

```python
import functools
import math

import jax
import jax.numpy as jnp
from jax import lax
from jax.experimental import pallas as pl
from jax.experimental.pallas import tpu as pltpu
from jax.sharding import PartitionSpec as P

EXPERTS = 8
TOPK = 3
STEPS = 2
CAP = 2
LANES = 128
WIDE = 256
PART_UNITS = (7, 7, 7, 7)
DOWN_UNITS = (7, 7, 7, 7)
PARTS = len(PART_UNITS)
DOWNS = len(DOWN_UNITS)


def slot_tables(step_tokens, step_ids, step_gates):
    tok_count = step_ids.shape[0]
    flat_ids = step_ids.reshape(tok_count * TOPK)
    expert_hit = (flat_ids[:, None] == jnp.arange(EXPERTS, dtype=jnp.int32)[None, :]).astype(
        jnp.int32
    )
    slot_rank = jnp.sum((jnp.cumsum(expert_hit, axis=0) - expert_hit) * expert_hit, axis=1)
    slot_index = flat_ids * CAP + slot_rank
    placed = (slot_index[:, None] == jnp.arange(EXPERTS * CAP, dtype=jnp.int32)[None, :]).astype(
        jnp.float32
    )
    selector = jnp.sum(placed.reshape(tok_count, TOPK, EXPERTS * CAP), axis=1)
    blocks = jnp.einsum(
        "ts,td->sd", selector.astype(jnp.bfloat16), step_tokens, preferred_element_type=jnp.float32
    ).astype(jnp.bfloat16)
    share_row = jnp.broadcast_to(
        (jnp.arange(TOPK) == 0).astype(jnp.float32)[None, :], (tok_count, TOPK)
    ).reshape(-1)
    gate_row = step_gates.astype(jnp.float32).reshape(-1)
    slot_coefs = jnp.einsum(
        "rs,rc->sc",
        placed,
        jnp.stack([gate_row, share_row], axis=1),
        precision=lax.Precision.HIGHEST,
    ).astype(jnp.bfloat16)
    return (blocks.reshape(EXPERTS, CAP, -1), slot_coefs.reshape(EXPERTS, CAP, 2), selector)


def send_out(blocks, slot_coefs, group_size):
    spread = jnp.repeat(blocks, group_size, axis=0)
    spread_coefs = jnp.repeat(slot_coefs, group_size, axis=0)
    arrived, arrived_coefs = (
        lax.all_to_all(spread, "fast", split_axis=0, concat_axis=0, tiled=True),
        lax.all_to_all(spread_coefs, "fast", split_axis=0, concat_axis=0, tiled=True),
    )
    return (arrived, arrived_coefs)


def expert_work(arrived, arrived_coefs, weights):
    w_gate_up, w_down, shared_gate_up, shared_down = weights
    model_width = arrived.shape[-1]
    hidden_size = w_down.shape[0]
    flat_rows = arrived.reshape(-1, model_width)
    flat_coef = arrived_coefs.reshape(-1, 2).astype(jnp.float32)
    row_count = flat_rows.shape[0]
    block_rows = math.gcd(row_count, 512)
    routed_up = w_gate_up.reshape(model_width, 2 * hidden_size)
    common_up = shared_gate_up.reshape(model_width, 2 * hidden_size)

    def one_block(block_pair):
        row_block, slot_coef = block_pair
        routed = jnp.dot(row_block, routed_up, preferred_element_type=jnp.float32)
        routed_hidden = (jax.nn.silu(routed[:, :hidden_size]) * routed[:, hidden_size:]).astype(
            jnp.bfloat16
        )
        common = jnp.dot(row_block, common_up, preferred_element_type=jnp.float32)
        common_hidden = (jax.nn.silu(common[:, :hidden_size]) * common[:, hidden_size:]).astype(
            jnp.bfloat16
        )
        result = slot_coef[:, 0:1] * jnp.dot(
            routed_hidden, w_down, preferred_element_type=jnp.float32
        )
        result = result + slot_coef[:, 1:2] * jnp.dot(
            common_hidden, shared_down, preferred_element_type=jnp.float32
        )
        return result.astype(jnp.bfloat16)

    outcome = lax.map(
        one_block,
        (flat_rows.reshape(-1, block_rows, model_width), flat_coef.reshape(-1, block_rows, 2)),
    )
    return outcome.reshape(arrived.shape)


def round_trip(blocks, slot_coefs, weights, group_size):
    arrived, arrived_coefs = send_out(blocks, slot_coefs, group_size)
    partials = expert_work(arrived, arrived_coefs, weights)
    returned = lax.all_to_all(partials, "fast", split_axis=0, concat_axis=0, tiled=True)
    slot_count = blocks.shape[1]
    return returned.reshape(EXPERTS, group_size, slot_count, -1).astype(jnp.float32).sum(axis=1)


def finish(selector, summed):
    flat_sums = summed.reshape(selector.shape[1], -1)
    return jnp.dot(
        selector, flat_sums, precision=lax.Precision.HIGHEST, preferred_element_type=jnp.float32
    ).astype(jnp.bfloat16)


def local_exchange(tokens, expert_ids, gate_weights, w_gate_up, w_down, shared_gate_up, shared_down):
    group_size = lax.axis_size("fast") // EXPERTS
    weights = (w_gate_up, w_down, shared_gate_up, shared_down)
    prepared = [
        slot_tables(tokens[step_index], expert_ids[step_index], gate_weights[step_index])
        for step_index in range(STEPS)
    ]
    outputs = []
    model_width = tokens.shape[-1]
    blocks = jnp.stack([member[0] for member in prepared], axis=1).reshape(
        EXPERTS, STEPS * CAP, model_width
    )
    slot_coefs = jnp.stack([member[1] for member in prepared], axis=1).reshape(
        EXPERTS, STEPS * CAP, 2
    )
    summed = round_trip(blocks, slot_coefs, weights, group_size).reshape(
        EXPERTS, STEPS, CAP, model_width
    )
    for step_index in range(STEPS):
        outputs.append(finish(prepared[step_index][2], summed[:, step_index]))
    return jnp.stack(outputs, axis=0)


def spans(size, units):
    unit = size // sum(units)
    return [(unit * sum(units[:i]), unit * count) for i, count in enumerate(units)]


def fused_kernel(
    n,
    tok_ref, ids_ref, gates_ref, wg_ref, wd_ref, sg_ref, sd_ref, out_ref,
    wb, wsb, x2, x2s, acc, accs, hid, hids, pick, mix,
    dsp, xr, xs, k1, s1, r1, s2, r2,
    up_sem, down_sem, d_send, d_recv, f_send, f_recv, sx_send, sx_recv, sc_send, sc_recv,
    c_send, c_recv, z_send, z_recv, x_send, x_recv, n_send, sn_send, sn_recv, y_send, y_recv,
):
    depth, _, units = wg_ref.shape
    steps, per_step, _ = tok_ref.shape
    rows = steps * per_step
    zs, chips = n // 4, n // 2
    slots = chips * rows
    tiles, share_tiles = units // LANES, units // (2 * LANES)
    share = share_tiles * LANES
    parts, downs = spans(depth, PART_UNITS), spans(depth, DOWN_UNITS)
    f = lax.axis_index("fast")
    core, xx, zz = f % 2, (f // 2) % 2, f // 4
    me = f // 2
    core_peer = {"fast": f + 1 - 2 * core}
    x_peer = {"fast": f + 2 - 4 * xx + 1 - 2 * core}
    away = [(dz, dx) for dz in range(1, zs) for dx in (0, 1)] + [(0, 1)]

    def chip_of(i):
        dz, dx = away[i]
        return ((zz + dz) % zs) * 2 + (xx + dx) % 2

    def peer_of(i):
        return {"fast": chip_of(i) * 2 + 1 - core}

    def remote(src, dst, ssem, rsem, peer):
        return pltpu.make_async_remote_copy(
            src_ref=src, dst_ref=dst, send_sem=ssem, recv_sem=rsem,
            device_id=peer, device_id_type=pl.DeviceIdType.MESH,
        )

    barrier = pltpu.get_barrier_semaphore()
    for peer in [core_peer] + [peer_of(i) for i in range(len(away))]:
        pl.semaphore_signal(barrier, inc=1, device_id=peer, device_id_type=pl.DeviceIdType.MESH)

    flat_g = wg_ref.reshape(2 * depth, units)
    flat_s = sg_ref.reshape(2 * depth, units)
    share_at = pl.multiple_of(xx * share, share)

    def up_copies(p):
        span = pl.ds(2 * parts[p][0], 2 * parts[p][1])
        for t in range(tiles):
            yield pltpu.make_async_copy(
                flat_g.at[span, pl.ds(t * LANES, LANES)], wb.at[t, span], up_sem.at[p, t]
            )
        for t in range(share_tiles):
            yield pltpu.make_async_copy(
                flat_s.at[span, pl.ds(share_at + t * LANES, LANES)],
                wsb.at[t, span],
                up_sem.at[p, tiles + t],
            )

    def down_place(c):
        return wb.at[c % tiles, pl.ds((c // tiles) * units, units)]

    def share_place(c):
        return wsb.at[c % share_tiles, pl.ds((c // share_tiles) * share, share)]

    def down_range(q):
        at, size = downs[q]
        return range(at // LANES, (at + size) // LANES)

    def down_copies(q):
        for i, c in enumerate(down_range(q)):
            cols = pl.ds(c * LANES, LANES)
            yield pltpu.make_async_copy(wd_ref.at[:, cols], down_place(c), down_sem.at[q, i])
            yield pltpu.make_async_copy(
                sd_ref.at[pl.ds(share_at, share), cols],
                share_place(c),
                down_sem.at[q, len(down_range(q)) + i],
            )

    def begin(copies):
        for copy in copies:
            copy.start()

    for p in range(PARTS):
        begin(up_copies(p))

    slot = lax.broadcasted_iota(jnp.int32, (slots, 2 * rows), 0)
    lane = lax.broadcasted_iota(jnp.int32, (slots, 2 * rows), 1)
    slot_expert, slot_step, slot_cap = slot // rows, slot % (rows // 2) // CAP, slot % CAP
    lane_step = lane % rows // per_step
    named = jnp.zeros((slots, 2 * rows), jnp.float32)
    gate = jnp.zeros((slots, 2 * rows), jnp.float32)
    for k in range(TOPK):
        ids = jnp.concatenate([ids_ref[k, s : s + 1, :] for s in range(steps)] * 2, axis=1)
        gates = gates_ref[k].astype(jnp.float32)
        gates = jnp.concatenate([gates[s : s + 1, :] for s in range(steps)] * 2, axis=1)
        match = ids == slot_expert
        named = named + jnp.where(match, 1.0, 0.0)
        gate = gate + jnp.where(match, gates, 0.0)
    before = lax.broadcasted_iota(jnp.int32, (2 * rows, 2 * rows), 0)
    after = lax.broadcasted_iota(jnp.int32, (2 * rows, 2 * rows), 1)
    earlier = jnp.where((before // per_step == after // per_step) & (before < after), 1.0, 0.0)
    rank = jnp.dot(
        named.astype(jnp.bfloat16), earlier.astype(jnp.bfloat16), preferred_element_type=jnp.float32
    )
    here = (rank == slot_cap.astype(jnp.float32)) & (lane_step == slot_step)
    placed = jnp.where(here, named, 0.0)
    gate = jnp.where(here, gate, 0.0)
    low = slot % rows < rows // 2
    weight = jnp.where((lane < rows) == low, gate, 0.0)
    eye_r = lax.broadcasted_iota(jnp.int32, (slots, slots), 0)
    eye_c = lax.broadcasted_iota(jnp.int32, (slots, slots), 1)
    eye = jnp.where(eye_r == eye_c, 1.0, 0.0).astype(jnp.bfloat16)
    mix[...] = lax.dot_general(
        weight.astype(jnp.bfloat16), eye, (((0,), (0,)), ((), ())), preferred_element_type=jnp.float32
    ).astype(jnp.bfloat16)
    own_r = lax.broadcasted_iota(jnp.int32, (rows, rows), 0)
    own_c = lax.broadcasted_iota(jnp.int32, (rows, rows), 1)
    pick[0:slots] = placed[:, :rows]
    pick[slots : slots + rows] = jnp.where(own_r == own_c, 1.0, 0.0)

    def halved(width):
        return lax.broadcasted_iota(jnp.int32, (slots, width), 0) % rows < rows // 2

    def lay_out(p):
        at, part = parts[p]
        half = part // 2
        chooser = pick[...].astype(jnp.bfloat16)
        x = jnp.concatenate(
            [tok_ref[s, :, at : at + part].astype(jnp.float32) for s in range(steps)], axis=0
        ).astype(jnp.bfloat16)
        a = jnp.dot(chooser, x[:, :half], preferred_element_type=jnp.float32)
        b = jnp.dot(chooser, x[:, half:], preferred_element_type=jnp.float32)
        block = jnp.where(halved(half), a[:slots], b[:slots]).reshape(chips, rows, half)
        dsp[p, :, :, 0:half] = block.astype(jnp.bfloat16)
        xs[p, core, xx, :, 0:half] = a[slots:].astype(jnp.bfloat16)
        xs[p, core, xx, :, half:part] = b[slots:].astype(jnp.bfloat16)

    def half_of(p):
        return pl.ds(0, parts[p][1] // 2)

    def part_of(p):
        return pl.ds(0, parts[p][1])

    def slot_send(p, i):
        return remote(
            dsp.at[p, chip_of(i), :, half_of(p)], xr.at[p, core, me, :, half_of(p)], d_send.at[p, i], d_recv.at[p, me], peer_of(i)
        )

    def share_send(p):
        return remote(
            xs.at[p, core, xx, :, part_of(p)], xs.at[p, core, xx, :, part_of(p)],
            sx_send.at[p], sx_recv.at[p], x_peer,
        )

    def slot_near(p):
        return remote(
            dsp.at[p, me, :, half_of(p)], xr.at[p, core, me, :, half_of(p)],
            n_send.at[p], d_recv.at[p, me], core_peer,
        )

    def share_near(p):
        block = xs.at[p, core, xx, :, part_of(p)]
        return remote(block, block, sn_send.at[p], sn_recv.at[p], core_peer)

    def slot_pass(p):
        block = xr.at[p, 1 - core, :, :, half_of(p)]
        return remote(block, block, f_send.at[p], f_recv.at[p], core_peer)

    def share_pass(p):
        block = xs.at[p, 1 - core, 1 - xx, :, part_of(p)]
        return remote(block, block, sc_send.at[p], sc_recv.at[p], core_peer)

    for p in range(PARTS):
        lay_out(p)
    pl.semaphore_wait(barrier, len(away) + 1)
    for p in range(PARTS):
        for i in range(len(away)):
            slot_send(p, i).start()
        share_send(p).start()
        slot_near(p).start()
        share_near(p).start()

    def landed(ref, sem):
        pltpu.make_async_copy(ref, ref, sem).wait()

    def forward(p):
        landed(xs.at[p, 1 - core, 1 - xx, :, part_of(p)], sx_recv.at[p])
        share_pass(p).start()
        for i in range(len(away)):
            landed(xr.at[p, 1 - core, chip_of(i), :, half_of(p)], d_recv.at[p, chip_of(i)])
        landed(xr.at[p, 1 - core, me, :, half_of(p)], d_recv.at[p, me])
        slot_pass(p).start()

    def settle(p):
        landed(xs.at[p, 1 - core, xx, :, part_of(p)], sn_recv.at[p])
        landed(xs.at[p, core, 1 - xx, :, part_of(p)], sc_recv.at[p])
        landed(xr.at[p, core, :, :, half_of(p)], f_recv.at[p])

    row_id = lax.broadcasted_iota(jnp.int32, (LANES, 2 * WIDE), 0)
    col_id = lax.broadcasted_iota(jnp.int32, (LANES, 2 * WIDE), 1)
    hit = (col_id == 2 * row_id) | (col_id == WIDE + 2 * row_id + 1)
    spread = jnp.where(hit, 1.0, 0.0).astype(jnp.bfloat16)
    first = lax.broadcasted_iota(jnp.int32, (slots, LANES), 0) % rows < rows // 2
    shared_rows = 4 * rows

    def expand(p):
        start, part = parts[p]
        half = part // 2
        for j in range(half // LANES):
            cols = slice(j * LANES, (j + 1) * LANES)
            b0 = xr[p, 0, :, :, cols].astype(jnp.float32).reshape(slots, LANES)
            b1 = xr[p, 1, :, :, cols].astype(jnp.float32).reshape(slots, LANES)
            pieces = [
                jnp.where(first, b0, pltpu.roll(b1, rows // 2, 0)),
                jnp.where(first, pltpu.roll(b0, slots - rows // 2, 0), b1),
            ]
            for h in range(2):
                at = h * half + j * LANES
                piece = xs[p, :, :, :, at : at + LANES].astype(jnp.float32)
                pieces.append(piece.reshape(shared_rows, LANES))
            mixed = jnp.concatenate(pieces, axis=0).astype(jnp.bfloat16)
            both = jnp.dot(mixed, spread, preferred_element_type=jnp.float32).astype(jnp.bfloat16)
            for h in range(2):
                to = 2 * (start + h * half + j * LANES)
                for g in range(2):
                    ways = slice(g * WIDE, (g + 1) * WIDE)
                    x2[g * slots : (g + 1) * slots, to : to + WIDE] = both[
                        h * slots : (h + 1) * slots, ways
                    ]
                    x2s[g * shared_rows : (g + 1) * shared_rows, to : to + WIDE] = both[
                        2 * slots + h * shared_rows : 2 * slots + (h + 1) * shared_rows, ways
                    ]

    def multiply(p):
        for copy in up_copies(p):
            copy.wait()
        span = pl.ds(2 * parts[p][0], 2 * parts[p][1])
        w = jnp.concatenate([wb[t, span] for t in range(tiles)], axis=1)
        d = jnp.dot(x2[:, span], w, preferred_element_type=jnp.float32)
        if p + 1 < PARTS:
            forward(p + 1)
        w = jnp.concatenate([wsb[t, span] for t in range(share_tiles)], axis=1)
        ds = jnp.dot(x2s[:, span], w, preferred_element_type=jnp.float32)
        if p == 0:
            acc[...] = d
            accs[...] = ds
        else:
            acc[...] += d
            accs[...] += ds

    def freed_by(q):
        end = (downs[q][0] + downs[q][1]) // LANES
        last = max(-(-end // tiles) * units, -(-end // share_tiles) * share)
        return next(p for p in range(PARTS) if 2 * sum(parts[p]) >= last)

    forward(0)
    for p in range(PARTS):
        settle(p)
        expand(p)
        multiply(p)
        for q in range(DOWNS):
            if freed_by(q) == p:
                begin(down_copies(q))

    def hidden(both, m):
        return (jax.nn.silu(both[:m]) * both[m:]).astype(jnp.bfloat16)

    hid[...] = hidden(acc[...], slots)
    hids[...] = hidden(accs[...], shared_rows)

    def wide_of(q):
        return pl.ds(0, downs[q][1] // 2)

    def core_copy(q):
        cols = wide_of(q)
        return remote(
            s1.at[q, :, cols], r1.at[q, :, cols], c_send.at[q], c_recv.at[q], core_peer
        )

    def slot_copy(q, i):
        return remote(
            s2.at[q, chip_of(i), :, wide_of(q)], r2.at[q, me, :, wide_of(q)],
            z_send.at[q, i], z_recv.at[q, me], peer_of(i),
        )

    def slot_home(q):
        return remote(
            s2.at[q, me, :, wide_of(q)], r2.at[q, me, :, wide_of(q)],
            z_send.at[q, len(away)], z_recv.at[q, me], core_peer,
        )

    def share_home(q):
        return remote(
            s2.at[q, pl.ds(chips + 2 * xx, 2), :, wide_of(q)],
            r2.at[q, pl.ds(chips + 2, 2), :, wide_of(q)],
            y_send.at[q], y_recv.at[q], core_peer,
        )

    def x_copy(q):
        return remote(
            s2.at[q, pl.ds(chips + 2 * (1 - xx), 2), :, wide_of(q)],
            r2.at[q, pl.ds(chips, 2), :, wide_of(q)],
            x_send.at[q],
            x_recv.at[q],
            x_peer,
        )

    mine = 2 * rows

    def stage_one(q):
        for copy in down_copies(q):
            copy.wait()
        cs, wide = down_range(q), downs[q][1] // 2
        top = halved(wide)
        w = jnp.concatenate([down_place(c)[...] for c in cs], axis=1)
        a = jnp.dot(hid[...], w, preferred_element_type=jnp.float32)
        w = jnp.concatenate([share_place(c)[...] for c in cs], axis=1)
        b = jnp.dot(hids[...], w, preferred_element_type=jnp.float32)
        lo, hi = a[:, :wide], a[:, wide:]
        t0 = jnp.where(top, lo, pltpu.roll(hi, rows // 2, 0))
        t1 = jnp.where(top, pltpu.roll(lo, slots - rows // 2, 0), hi)

        def pack(t, u):
            return jnp.concatenate(
                [t, u[:rows, :wide], u[:rows, wide:], u[rows:, :wide], u[rows:, wide:]], axis=0
            )

        p0, p1 = pack(t0, b[:mine]), pack(t1, b[mine:])
        s1[q, :, 0:wide] = jnp.where(core == 0, p0, p1).astype(jnp.bfloat16)
        core_copy(q).start()
        k1[q, :, 0:wide] = jnp.where(core == 0, p1, p0)

    def stage_two(q):
        core_copy(q).wait_recv()
        wide = downs[q][1] // 2
        p = k1[q, :, 0:wide] + r1[q, :, 0:wide].astype(jnp.float32)
        s2[q, :, :, 0:wide] = p.reshape(chips + 4, rows, wide).astype(jnp.bfloat16)
        for i in range(len(away)):
            slot_copy(q, i).start()
        x_copy(q).start()
        slot_home(q).start()
        share_home(q).start()

    def stage_three(q):
        at, wide = downs[q][0], downs[q][1] // 2
        for i in range(len(away)):
            landed(r2.at[q, chip_of(i), :, wide_of(q)], z_recv.at[q, chip_of(i)])
        landed(r2.at[q, me, :, wide_of(q)], z_recv.at[q, me])
        x_copy(q).wait_recv()
        share_home(q).wait_recv()
        back = r2[q, 0:chips, :, 0:wide].astype(jnp.float32).reshape(slots, wide).astype(jnp.bfloat16)
        both = jnp.dot(mix[...], back, preferred_element_type=jnp.float32)
        for h in range(2):
            p = both[h * rows : (h + 1) * rows]
            p = p + r2[q, chips + h, :, 0:wide].astype(jnp.float32)
            p = p + r2[q, chips + 2 + h, :, 0:wide].astype(jnp.float32)
            p = p.astype(jnp.bfloat16).astype(jnp.float32)
            to = at + h * wide
            for s in range(steps):
                out_ref[s, :, to : to + wide] = p[s * per_step : (s + 1) * per_step].astype(
                    jnp.bfloat16
                )

    for step in range(DOWNS + 2):
        if step >= 2:
            stage_two(step - 2)
        if step < DOWNS:
            stage_one(step)
    def sent(q):
        for copy in (x_copy(q), slot_home(q), share_home(q)):
            copy.wait_send()
        for i in range(len(away)):
            slot_copy(q, i).wait_send()

    for p in range(PARTS):
        for i in range(len(away)):
            slot_send(p, i).wait_send()
        for copy in (share_send(p), slot_pass(p), share_pass(p), slot_near(p), share_near(p)):
            copy.wait_send()
    for q in range(DOWNS):
        core_copy(q).wait_send()
        if q + 1 < DOWNS:
            sent(q)
    for q in range(DOWNS):
        stage_three(q)
    sent(DOWNS - 1)


def scratch_of(n, rows, depth, units):
    chips = n // 2
    slots, shared = chips * rows, 4 * rows
    tiles, share_tiles = units // LANES, units // (2 * LANES)
    part = max(size for _, size in spans(depth, PART_UNITS))
    down = max(size for _, size in spans(depth, DOWN_UNITS))
    half, wide, down_tiles = part // 2, down // 2, down // LANES
    bf, fl = jnp.bfloat16, jnp.float32
    packed = slots + 4 * rows
    buffers = [
        ((tiles, 2 * depth, LANES), bf),
        ((share_tiles, 2 * depth, LANES), bf),
        ((2 * slots, 2 * depth), bf),
        ((2 * shared, 2 * depth), bf),
        ((2 * slots, units), fl),
        ((2 * shared, share_tiles * LANES), fl),
        ((slots, units), bf),
        ((shared, share_tiles * LANES), bf),
        ((slots + rows, rows), fl),
        ((2 * rows, slots), bf),
        ((PARTS, chips, rows, half), bf),
        ((PARTS, 2, chips, rows, half), bf),
        ((PARTS, 2, 2, rows, part), bf),
        ((DOWNS, packed, wide), fl),
        ((DOWNS, packed, wide), bf),
        ((DOWNS, packed, wide), bf),
        ((DOWNS, chips + 4, rows, wide), bf),
        ((DOWNS, chips + 4, rows, wide), bf),
    ]
    dma = pltpu.SemaphoreType.DMA
    sems = [
        dma((PARTS, tiles + share_tiles)), dma((DOWNS, 2 * down_tiles)),
        dma((PARTS, chips)), dma((PARTS, chips)),
        dma((PARTS,)), dma((PARTS,)), dma((PARTS,)), dma((PARTS,)), dma((PARTS,)), dma((PARTS,)),
        dma((DOWNS,)), dma((DOWNS,)), dma((DOWNS, chips)), dma((DOWNS, chips)),
        dma((DOWNS,)), dma((DOWNS,)), dma((PARTS,)), dma((PARTS,)), dma((PARTS,)),
        dma((DOWNS,)), dma((DOWNS,)),
    ]
    return [pltpu.VMEM(shape, kind) for shape, kind in buffers] + sems


def local_fused(tokens, expert_ids, gate_weights, w_gate_up, w_down, shared_gate_up, shared_down):
    n = lax.axis_size("fast")
    steps, per_step, depth = tokens.shape
    rows, units = steps * per_step, w_gate_up.shape[2]
    whole = pl.BlockSpec(memory_space=pltpu.VMEM)
    there = pl.BlockSpec(memory_space=pl.ANY)
    return pl.pallas_call(
        functools.partial(fused_kernel, n),
        out_shape=jax.ShapeDtypeStruct((steps, per_step, depth), jnp.bfloat16),
        in_specs=[whole, whole, whole, there, there, there, there],
        out_specs=whole,
        scratch_shapes=scratch_of(n, rows, depth, units),
        compiler_params=pltpu.CompilerParams(
            collective_id=0, has_side_effects=True, vmem_limit_bytes=67043328
        ),
    )(
        tokens,
        jnp.transpose(expert_ids, (2, 0, 1)),
        jnp.transpose(gate_weights, (2, 0, 1)),
        w_gate_up, w_down, shared_gate_up, shared_down,
    )


def local(tokens, expert_ids, gate_weights, w_gate_up, w_down, shared_gate_up, shared_down):
    n = lax.axis_size("fast")
    steps, per_step, depth = tokens.shape
    units = w_gate_up.shape[2]
    fits = n == 2 * EXPERTS and steps == STEPS and per_step == 2 * CAP
    fits = fits and units == EXPERTS * LANES and depth == 2 * LANES * sum(PART_UNITS) == 2 * LANES * sum(DOWN_UNITS)
    run = local_fused if fits else local_exchange
    return run(
        tokens, expert_ids, gate_weights, w_gate_up, w_down, shared_gate_up, shared_down
    )


def solution(mesh):
    placed = (
        P(None, ("rep", "fast"), None),
        P(None, ("rep", "fast"), None),
        P(None, ("rep", "fast"), None),
        P(None, None, "fast"),
        P("fast", None),
        P(None, None, "fast"),
        P("fast", None),
    )
    return jax.shard_map(
        local, mesh=mesh, in_specs=placed, out_specs=P(None, ("rep", "fast"), None), check_vma=False
    )
```
